256 devices in a mesh: dp: 4 (over x), blk: 16 (over z_lo, y, core), mp: 4 (over z_hi).
Axes of the slice: x: 4, y: 4, z: 8 (z_hi: 4, z_lo: 2; z = z_hi * 2 + z_lo), core: 2. Of those that a mesh axis runs over, the one named last changes fastest.
Arguments:
- tokens: bfloat16 [16384, 7168], P('dp', ('blk', 'mp')), may hold values from -6 to 6
- trainer_q: float32 [3584, 7168], P(('mp', 'blk'), 'dp'), may hold values from -0.0625 to 0.0625
- kv_pool: bfloat16 [2, 8192, 3584], P(None, ('dp', 'blk'), 'mp')
- prompt_kv: bfloat16 [2, 16384, 3584], P(None, ('dp', 'blk'), 'mp'), may hold values from -15 to 15
- page_table: int32 [64, 64], P(('dp', 'blk')), may hold values from 0 to 127, as said below
- page_count: int32 [64], P(('dp', 'blk')), may hold values from 1 to 64
- prompt_len: int32 [64], P(('dp', 'blk')), may hold values from 64 to 256
Outputs:
- server_q: bfloat16 [3584, 7168], P('mp', 'blk')
- attn_out: bfloat16 [16384, 3584], P(('dp', 'blk'), 'mp')
The draws below stay inside these ranges and needn't reach their ends.
Inputs may be any that keep to these rules, and one draw needn't show every extreme that they name: `page_table`: the entries of a row are distinct page numbers of the request's group.
All inputs are finite; a program needn't handle non-finite values.
Results may differ from the reference program's by a relative error of at most 0.012.
The reference program's roundings to bfloat16 on the way count: a program that leaves them out, or rounds other values in their place, can miss the bound.
Values may be sent and summed in bfloat16 or wider, within the bound.
A program may use at most 128 MiB of HBM per device.

```python
import jax
import jax.numpy as jnp
from jax import lax

D = 7168
HEADS = 16
HD = 224
LEN = 256
PAGE = 16
HC = 3584
GROUPS = 4
GROUP_REQS = 16
REQUESTS = 64
TOKENS = 16384
GROUP_PAGES = 128
MAXP = 64
POOL_TOK = 8192


def draw_kv_pool(key, part):
    shape = (2, POOL_TOK, HC)
    values = 2.5 * jax.random.normal(key, shape, jnp.float32)
    return jnp.clip(values, -15.0, 15.0).astype(jnp.bfloat16)


def draw_page_table(key, part):
    row_keys = jax.random.split(key, REQUESTS)

    def one_row(row_key):
        return jax.random.permutation(row_key, GROUP_PAGES)[:MAXP]
    return jax.vmap(one_row)(row_keys).astype(jnp.int32)


def draw_page_count(key, part):
    first_key, second_key, third_key, fourth_key = jax.random.split(key, 4)
    first = jax.random.randint(first_key, (REQUESTS,), 0, MAXP)
    second = jax.random.randint(second_key, (REQUESTS,), 0, MAXP)
    third = jax.random.randint(third_key, (REQUESTS,), 0, MAXP)
    counts = 1 + first * second * third // (MAXP * MAXP)
    fullest = jax.random.randint(fourth_key, (), 0, REQUESTS)
    counts = jnp.where(jnp.arange(REQUESTS) == fullest, MAXP, counts)
    return counts.astype(jnp.int32)


def draw_prompt_len(key, part):
    first_key, second_key = jax.random.split(key)
    lengths = jax.random.randint(first_key, (REQUESTS,), LEN // 4, LEN + 1)
    longest = jax.random.randint(second_key, (), 0, REQUESTS)
    lengths = jnp.where(jnp.arange(REQUESTS) == longest, LEN, lengths)
    return lengths.astype(jnp.int32)


def block_scale(rng, dims, shards, least, high):
    gain, own = 1.0, jax.random.fold_in(rng, 6)
    for axis_at, parts in shards:
        steps = jnp.exp(jax.random.uniform(jax.random.fold_in(own, axis_at), (parts,), jnp.float32, least / len(shards), high / len(shards)))
        gain = gain * jnp.repeat(steps, dims[axis_at] // parts).reshape([-1 if axis == axis_at else 1 for axis in range(len(dims))])
    return gain


def scatter_about(own_key, dims, width, most, shards=(), held_as=jnp.bfloat16):
    drawn = width * jax.random.normal(own_key, dims, jnp.float32)
    if shards:
        drawn = drawn * block_scale(own_key, dims, shards, -0.22, 0.18)
    return jnp.clip(drawn, -most, most).astype(held_as)


def setup_inputs(seed: int = 0) -> dict:
    key_list = jax.random.split(jax.random.key(seed), 8)
    tokens = scatter_about(key_list[0], (TOKENS, D), 1.0, 6.0, ((0, 4), (1, 64)))
    trainer_q = scatter_about(key_list[1], (HC, D), D ** -0.5, 0.0625, ((0, 64), (1, 4)), jnp.float32)
    kv_pool = draw_kv_pool(jax.random.fold_in(key_list[7], 71), 0)
    prompt_kv = scatter_about(key_list[3], (2, TOKENS, HC), 2.5, 15.0, ((1, 64), (2, 4)))
    page_table = draw_page_table(jax.random.fold_in(key_list[7], 71), 0)
    page_count = draw_page_count(jax.random.fold_in(key_list[7], 71), 0)
    prompt_len = draw_prompt_len(jax.random.fold_in(key_list[7], 71), 0)
    return {"tokens": tokens, "trainer_q": trainer_q, "kv_pool": kv_pool, "prompt_kv": prompt_kv, "page_table": page_table, "page_count": page_count, "prompt_len": prompt_len}


very_negative = -1e30


def one_request(request_item, pool_keys, pool_values):
    queries, own_keys, own_values, row_pages, page_total, length, group_index = request_item
    query_heads = queries.reshape(LEN, HEADS, HD).astype(jnp.float32)
    group_keys = lax.dynamic_index_in_dim(pool_keys, group_index, 0, keepdims=False)
    group_values = lax.dynamic_index_in_dim(pool_values, group_index, 0, keepdims=False)
    key_heads = jnp.concatenate([own_keys, group_keys], 0).reshape(-1, HEADS, HD).astype(jnp.float32)
    value_heads = jnp.concatenate([own_values, group_values], 0).reshape(-1, HEADS, HD).astype(jnp.float32)
    page_ids = jnp.arange(GROUP_PAGES * PAGE, dtype=jnp.int32) // PAGE
    live_slots = jnp.arange(MAXP, dtype=jnp.int32) < page_total
    page_used = jnp.any((row_pages[None, :] == page_ids[:, None]) & live_slots[None, :], axis=1)
    row_index = jnp.arange(LEN, dtype=jnp.int32)
    own_mask = (row_index[None, :] <= row_index[:, None]) & (row_index[None, :] < length)
    pool_mask = jnp.broadcast_to(page_used[None, :], (LEN, GROUP_PAGES * PAGE))
    key_mask = jnp.concatenate([own_mask, pool_mask], 1)
    scores = jnp.einsum("thd,khd->htk", query_heads, key_heads) * (HD ** -0.5)
    scores = jnp.where(key_mask[None], scores, very_negative)
    largest = jnp.max(scores, axis=2, keepdims=True)
    weights = jnp.where(key_mask[None], jnp.exp(scores - largest), 0.0)
    row_total = jnp.sum(weights, axis=2)
    rounded = lax.optimization_barrier(weights.astype(jnp.bfloat16)).astype(jnp.float32)
    mixed = jnp.einsum("htk,khd->htd", rounded, value_heads) / row_total[:, :, None]
    mixed = jnp.where((row_index < length)[None, :, None], mixed, 0.0)
    return jnp.transpose(mixed, (1, 0, 2)).reshape(LEN, HEADS * HD).astype(jnp.bfloat16)


def reference(tokens, trainer_q, kv_pool, prompt_kv, page_table, page_count, prompt_len):
    server_q = trainer_q.astype(jnp.bfloat16)
    queries = jnp.dot(tokens, server_q.T, preferred_element_type=jnp.float32).astype(jnp.bfloat16)
    pool_keys = kv_pool[0].reshape(GROUPS, GROUP_PAGES * PAGE, HC)
    pool_values = kv_pool[1].reshape(GROUPS, GROUP_PAGES * PAGE, HC)
    items = (queries.reshape(REQUESTS, LEN, HC),
             prompt_kv[0].reshape(REQUESTS, LEN, HC),
             prompt_kv[1].reshape(REQUESTS, LEN, HC),
             page_table, page_count, prompt_len,
             jnp.arange(REQUESTS, dtype=jnp.int32) // GROUP_REQS)
    mixed = lax.map(lambda request_item: one_request(request_item, pool_keys, pool_values), items)
    return server_q, mixed.reshape(TOKENS, HC)
```

```python
import jax
import jax.numpy as jnp
from jax import lax
from jax.sharding import PartitionSpec as P

HD = 224
PAGE = 16


def attend_block(softmax_state, query_heads, key_heads, value_heads, key_mask):
    running_max, row_total, weighted = softmax_state
    scores = jnp.einsum(
        "thd,khd->htk", query_heads, key_heads, preferred_element_type=jnp.float32
    ) * HD ** (-0.5)
    scores = jnp.where(key_mask[None], scores, -1e30)
    new_max = jnp.maximum(running_max, jnp.max(scores, axis=2))
    weights = jnp.where(key_mask[None], jnp.exp(scores - new_max[:, :, None]), 0.0)
    factor = jnp.exp(running_max - new_max)
    row_total = row_total * factor + jnp.sum(weights, axis=2)
    weighted = weighted * factor[:, :, None] + jnp.einsum(
        "htk,khd->htd",
        weights.astype(jnp.bfloat16),
        value_heads,
        preferred_element_type=jnp.float32,
    )
    return (new_max, row_total, weighted)


def body(tokens, trainer_q, kv_pool, prompt_kv, page_table, page_count, prompt_len):
    blk_size = lax.axis_size("blk")
    mp_size = lax.axis_size("mp")
    trainer_rows = lax.all_gather(trainer_q.astype(jnp.bfloat16), "dp", axis=1, tiled=True)
    head_weights = lax.all_gather(trainer_rows, "blk", axis=0, tiled=True)
    head_width, model_width = head_weights.shape
    block_cols = model_width // blk_size
    server_q = lax.dynamic_slice_in_dim(
        head_weights, lax.axis_index("blk") * block_cols, block_cols, axis=1
    )
    group_rows, piece_cols = tokens.shape
    own_rows = group_rows // blk_size
    pieces = tokens.reshape(blk_size, 1, own_rows, piece_cols)
    pieces = jnp.broadcast_to(pieces, (blk_size, mp_size, own_rows, piece_cols))
    pieces = pieces.reshape(blk_size * mp_size, own_rows, piece_cols)
    pieces = lax.all_to_all(pieces, ("blk", "mp"), 0, 0, tiled=True)
    token_local = jnp.transpose(pieces, (1, 0, 2)).reshape(own_rows, -1)
    queries = jnp.einsum(
        "td,hd->th", token_local, head_weights, preferred_element_type=jnp.float32
    )
    queries = queries.astype(jnp.bfloat16)
    head_count = head_width // HD
    query_heads = queries.reshape(own_rows, head_count, HD)
    length = prompt_len[0]
    row_pages = page_table[0]
    live_slots = jnp.arange(row_pages.shape[0], dtype=jnp.int32) < page_count[0]
    row_index = jnp.arange(own_rows, dtype=jnp.int32)
    own_mask = (row_index[None, :] <= row_index[:, None]) & (row_index[None, :] < length)
    softmax_state = (
        jnp.full((head_count, own_rows), -1e30, jnp.float32),
        jnp.zeros((head_count, own_rows), jnp.float32),
        jnp.zeros((head_count, own_rows, HD), jnp.float32),
    )
    softmax_state = attend_block(
        softmax_state,
        query_heads,
        prompt_kv[0].reshape(own_rows, head_count, HD),
        prompt_kv[1].reshape(own_rows, head_count, HD),
        own_mask,
    )
    shard_piece = lax.all_gather(kv_pool, "blk", axis=1, tiled=True)
    key_count = shard_piece.shape[1]
    page_ids = jnp.arange(key_count, dtype=jnp.int32) // PAGE
    page_used = jnp.any((row_pages[None, :] == page_ids[:, None]) & live_slots[None, :], axis=1)
    key_mask = jnp.broadcast_to(page_used[None, :], (own_rows, key_count))
    running_max, row_total, weighted = attend_block(
        softmax_state,
        query_heads,
        shard_piece[0].reshape(key_count, head_count, HD),
        shard_piece[1].reshape(key_count, head_count, HD),
        key_mask,
    )
    mixed = weighted / row_total[:, :, None]
    mixed = jnp.where((row_index < length)[None, :, None], mixed, 0.0)
    mixed = jnp.transpose(mixed, (1, 0, 2)).reshape(own_rows, head_width).astype(jnp.bfloat16)
    return (server_q, mixed)


def solution(mesh):
    in_specs = (
        P("dp", ("blk", "mp")),
        P(("mp", "blk"), "dp"),
        P(None, ("dp", "blk"), "mp"),
        P(None, ("dp", "blk"), "mp"),
        P(("dp", "blk"), None),
        P(("dp", "blk")),
        P(("dp", "blk")),
    )
    out_specs = (P("mp", "blk"), P(("dp", "blk"), "mp"))
    return jax.shard_map(body, mesh=mesh, in_specs=in_specs, out_specs=out_specs, check_vma=False)
```

```python
import jax
import jax.numpy as jnp
from jax import lax
from jax.sharding import PartitionSpec as P

HD = 224
PAGE = 16


def attend_block(softmax_state, query_heads, key_heads, value_heads, key_mask):
    running_max, row_total, weighted = softmax_state
    scores = jnp.einsum(
        "thd,khd->htk", query_heads, key_heads, preferred_element_type=jnp.float32
    ) * HD ** (-0.5)
    scores = jnp.where(key_mask[None], scores, -1e30)
    new_max = jnp.maximum(running_max, jnp.max(scores, axis=2))
    weights = jnp.where(key_mask[None], jnp.exp(scores - new_max[:, :, None]), 0.0)
    factor = jnp.exp(running_max - new_max)
    row_total = row_total * factor + jnp.sum(weights, axis=2)
    weighted = weighted * factor[:, :, None] + jnp.einsum(
        "htk,khd->htd",
        weights.astype(jnp.bfloat16),
        value_heads,
        preferred_element_type=jnp.float32,
    )
    return (new_max, row_total, weighted)


def blk_index():
    return lax.axis_index("chips") * lax.axis_size("core") + lax.axis_index("core")


def gather_blk(x, axis):
    parts = lax.all_gather(x, "chips", axis=0)
    parts = lax.all_gather(parts, "core", axis=1)
    parts = jnp.moveaxis(parts.reshape((-1,) + x.shape), 0, axis)
    shape = list(x.shape)
    shape[axis] = -1
    return parts.reshape(shape)


def body(tokens, trainer_q, kv_pool, prompt_kv, page_table, page_count, prompt_len):
    blk_size = lax.axis_size("chips") * lax.axis_size("core")
    mp_size = lax.axis_size("mp")
    trainer_rows = lax.all_gather(trainer_q.astype(jnp.bfloat16), "dp", axis=1, tiled=True)
    head_weights = gather_blk(trainer_rows, 0)
    head_width, model_width = head_weights.shape
    block_cols = model_width // blk_size
    server_q = lax.dynamic_slice_in_dim(
        head_weights, blk_index() * block_cols, block_cols, axis=1
    )
    group_rows, piece_cols = tokens.shape
    own_rows = group_rows // blk_size
    pieces = tokens.reshape(blk_size, 1, own_rows, piece_cols)
    pieces = jnp.broadcast_to(pieces, (blk_size, mp_size, own_rows, piece_cols))
    pieces = pieces.reshape(blk_size * mp_size, own_rows, piece_cols)
    pieces = lax.all_to_all(pieces, ("chips", "core", "mp"), 0, 0, tiled=True)
    token_local = jnp.transpose(pieces, (1, 0, 2)).reshape(own_rows, -1)
    queries = jnp.einsum(
        "td,hd->th", token_local, head_weights, preferred_element_type=jnp.float32
    )
    queries = queries.astype(jnp.bfloat16)
    head_count = head_width // HD
    query_heads = queries.reshape(own_rows, head_count, HD)
    length = prompt_len[0]
    row_pages = page_table[0]
    live_slots = jnp.arange(row_pages.shape[0], dtype=jnp.int32) < page_count[0]
    row_index = jnp.arange(own_rows, dtype=jnp.int32)
    own_mask = (row_index[None, :] <= row_index[:, None]) & (row_index[None, :] < length)
    softmax_state = (
        jnp.full((head_count, own_rows), -1e30, jnp.float32),
        jnp.zeros((head_count, own_rows), jnp.float32),
        jnp.zeros((head_count, own_rows, HD), jnp.float32),
    )
    softmax_state = attend_block(
        softmax_state,
        query_heads,
        prompt_kv[0].reshape(own_rows, head_count, HD),
        prompt_kv[1].reshape(own_rows, head_count, HD),
        own_mask,
    )
    shard_piece = gather_blk(kv_pool, 1)
    key_count = shard_piece.shape[1]
    page_ids = jnp.arange(key_count, dtype=jnp.int32) // PAGE
    page_used = jnp.any((row_pages[None, :] == page_ids[:, None]) & live_slots[None, :], axis=1)
    key_mask = jnp.broadcast_to(page_used[None, :], (own_rows, key_count))
    running_max, row_total, weighted = attend_block(
        softmax_state,
        query_heads,
        shard_piece[0].reshape(key_count, head_count, HD),
        shard_piece[1].reshape(key_count, head_count, HD),
        key_mask,
    )
    mixed = weighted / row_total[:, :, None]
    mixed = jnp.where((row_index < length)[None, :, None], mixed, 0.0)
    mixed = jnp.transpose(mixed, (1, 0, 2)).reshape(own_rows, head_width).astype(jnp.bfloat16)
    return (server_q, mixed)


def solution(mesh):
    dp_size, blk_size, mp_size = mesh.devices.shape
    fine = jax.sharding.Mesh(
        mesh.devices.reshape(dp_size, blk_size // 2, 2, mp_size), ("dp", "chips", "core", "mp")
    )
    blk = ("chips", "core")
    in_specs = (
        P("dp", blk + ("mp",)),
        P(("mp",) + blk, "dp"),
        P(None, ("dp",) + blk, "mp"),
        P(None, ("dp",) + blk, "mp"),
        P(("dp",) + blk, None),
        P(("dp",) + blk),
        P(("dp",) + blk),
    )
    out_specs = (P("mp", blk), P(("dp",) + blk, "mp"))
    return jax.shard_map(body, mesh=fine, in_specs=in_specs, out_specs=out_specs, check_vma=False)
```

```python
import jax
import jax.numpy as jnp
from jax import lax
from jax.sharding import PartitionSpec as P

HD = 224
PAGE = 16


def attend_block(softmax_state, query_heads, key_heads, value_heads, key_mask):
    running_max, row_total, weighted = softmax_state
    scores = jnp.einsum(
        "thd,khd->htk", query_heads, key_heads, preferred_element_type=jnp.float32
    ) * HD ** (-0.5)
    scores = jnp.where(key_mask[None], scores, -1e30)
    new_max = jnp.maximum(running_max, jnp.max(scores, axis=2))
    weights = jnp.where(key_mask[None], jnp.exp(scores - new_max[:, :, None]), 0.0)
    factor = jnp.exp(running_max - new_max)
    row_total = row_total * factor + jnp.sum(weights, axis=2)
    weighted = weighted * factor[:, :, None] + jnp.einsum(
        "htk,khd->htd",
        weights.astype(jnp.bfloat16),
        value_heads,
        preferred_element_type=jnp.float32,
    )
    return (new_max, row_total, weighted)


def body(tokens, trainer_q, kv_pool, prompt_kv, page_table, page_count, prompt_len):
    blk_size = lax.axis_size("blk")
    mp_size = lax.axis_size("mp")
    dp_size = lax.axis_size("dp")
    quarter = lax.all_gather(trainer_q.astype(jnp.bfloat16), "blk", axis=0, tiled=True)
    head_width, quarter_cols = quarter.shape
    quarter = jnp.broadcast_to(quarter[None], (dp_size, head_width, quarter_cols))
    quarters = lax.all_to_all(quarter, "dp", 0, 0, tiled=True)
    block_cols = quarter_cols * dp_size // blk_size
    blocks_per_quarter = quarter_cols // block_cols
    b = lax.axis_index("blk")
    server_q = lax.dynamic_slice(
        quarters,
        (b // blocks_per_quarter, 0, (b % blocks_per_quarter) * block_cols),
        (1, head_width, block_cols),
    )[0]
    group_rows, piece_cols = tokens.shape
    own_rows = group_rows // blk_size
    pieces = tokens.reshape(blk_size, 1, own_rows, piece_cols)
    pieces = jnp.broadcast_to(pieces, (blk_size, mp_size, own_rows, piece_cols))
    pieces = pieces.reshape(blk_size * mp_size, own_rows, piece_cols)
    pieces = lax.all_to_all(pieces, ("blk", "mp"), 0, 0, tiled=True)
    token_local = jnp.transpose(pieces, (1, 0, 2)).reshape(own_rows, -1)
    queries = jnp.einsum(
        "tgd,ghd->th",
        token_local.reshape(own_rows, dp_size, quarter_cols),
        quarters,
        preferred_element_type=jnp.float32,
    )
    queries = queries.astype(jnp.bfloat16)
    head_count = head_width // HD
    query_heads = queries.reshape(own_rows, head_count, HD)
    length = prompt_len[0]
    row_pages = page_table[0]
    live_slots = jnp.arange(row_pages.shape[0], dtype=jnp.int32) < page_count[0]
    row_index = jnp.arange(own_rows, dtype=jnp.int32)
    own_mask = (row_index[None, :] <= row_index[:, None]) & (row_index[None, :] < length)
    softmax_state = (
        jnp.full((head_count, own_rows), -1e30, jnp.float32),
        jnp.zeros((head_count, own_rows), jnp.float32),
        jnp.zeros((head_count, own_rows, HD), jnp.float32),
    )
    softmax_state = attend_block(
        softmax_state,
        query_heads,
        prompt_kv[0].reshape(own_rows, head_count, HD),
        prompt_kv[1].reshape(own_rows, head_count, HD),
        own_mask,
    )
    shard_piece = lax.all_gather(kv_pool, "blk", axis=1, tiled=True)
    key_count = shard_piece.shape[1]
    page_ids = jnp.arange(key_count, dtype=jnp.int32) // PAGE
    page_used = jnp.any((row_pages[None, :] == page_ids[:, None]) & live_slots[None, :], axis=1)
    key_mask = jnp.broadcast_to(page_used[None, :], (own_rows, key_count))
    running_max, row_total, weighted = attend_block(
        softmax_state,
        query_heads,
        shard_piece[0].reshape(key_count, head_count, HD),
        shard_piece[1].reshape(key_count, head_count, HD),
        key_mask,
    )
    mixed = weighted / row_total[:, :, None]
    mixed = jnp.where((row_index < length)[None, :, None], mixed, 0.0)
    mixed = jnp.transpose(mixed, (1, 0, 2)).reshape(own_rows, head_width).astype(jnp.bfloat16)
    return (server_q, mixed)


def solution(mesh):
    in_specs = (
        P("dp", ("blk", "mp")),
        P(("mp", "blk"), "dp"),
        P(None, ("dp", "blk"), "mp"),
        P(None, ("dp", "blk"), "mp"),
        P(("dp", "blk"), None),
        P(("dp", "blk")),
        P(("dp", "blk")),
    )
    out_specs = (P("mp", "blk"), P(("dp", "blk"), "mp"))
    return jax.shard_map(body, mesh=mesh, in_specs=in_specs, out_specs=out_specs, check_vma=False)
```

```python
import jax
import jax.numpy as jnp
from jax import lax
from jax.sharding import PartitionSpec as P

HD = 224
PAGE = 16


def attend_block(softmax_state, query_heads, key_heads, value_heads, key_mask):
    running_max, row_total, weighted = softmax_state
    scores = jnp.einsum(
        "thd,khd->htk", query_heads, key_heads, preferred_element_type=jnp.float32
    ) * HD ** (-0.5)
    scores = jnp.where(key_mask[None], scores, -1e30)
    new_max = jnp.maximum(running_max, jnp.max(scores, axis=2))
    weights = jnp.where(key_mask[None], jnp.exp(scores - new_max[:, :, None]), 0.0)
    factor = jnp.exp(running_max - new_max)
    row_total = row_total * factor + jnp.sum(weights, axis=2)
    weighted = weighted * factor[:, :, None] + jnp.einsum(
        "htk,khd->htd",
        weights.astype(jnp.bfloat16),
        value_heads,
        preferred_element_type=jnp.float32,
    )
    return (new_max, row_total, weighted)


def body(tokens, trainer_q, kv_pool, prompt_kv, page_table, page_count, prompt_len):
    blk_size = lax.axis_size("blk")
    mp_size = lax.axis_size("mp")
    trainer_rows = lax.all_gather(trainer_q.astype(jnp.bfloat16), "dp", axis=1, tiled=True)
    head_weights = lax.all_gather(trainer_rows, "blk", axis=0, tiled=True)
    head_width, model_width = head_weights.shape
    block_cols = model_width // blk_size
    server_q = lax.dynamic_slice_in_dim(
        head_weights, lax.axis_index("blk") * block_cols, block_cols, axis=1
    )
    group_rows, piece_cols = tokens.shape
    own_rows = group_rows // blk_size
    pieces = tokens.reshape(blk_size, 1, own_rows, piece_cols)
    pieces = jnp.broadcast_to(pieces, (blk_size, mp_size, own_rows, piece_cols))
    pieces = pieces.reshape(blk_size * mp_size, own_rows, piece_cols)
    pieces = lax.all_to_all(pieces, ("blk", "mp"), 0, 0, tiled=True)
    token_local = jnp.transpose(pieces, (1, 0, 2)).reshape(own_rows, -1)
    queries = jnp.einsum(
        "td,hd->th", token_local, head_weights, preferred_element_type=jnp.float32
    )
    queries = queries.astype(jnp.bfloat16)
    head_count = head_width // HD
    query_heads = queries.reshape(own_rows, head_count, HD)
    length = prompt_len[0]
    row_pages = page_table[0]
    live_slots = jnp.arange(row_pages.shape[0], dtype=jnp.int32) < page_count[0]
    row_index = jnp.arange(own_rows, dtype=jnp.int32)
    own_mask = (row_index[None, :] <= row_index[:, None]) & (row_index[None, :] < length)
    softmax_state = (
        jnp.full((head_count, own_rows), -1e30, jnp.float32),
        jnp.zeros((head_count, own_rows), jnp.float32),
        jnp.zeros((head_count, own_rows, HD), jnp.float32),
    )
    softmax_state = attend_block(
        softmax_state,
        query_heads,
        prompt_kv[0].reshape(own_rows, head_count, HD),
        prompt_kv[1].reshape(own_rows, head_count, HD),
        own_mask,
    )
    kv_pieces = jnp.broadcast_to(kv_pool[None], (blk_size,) + kv_pool.shape)
    kv_pieces = lax.all_to_all(kv_pieces, "blk", 0, 0, tiled=True)
    shard_piece = jnp.moveaxis(kv_pieces, 0, 1).reshape(
        kv_pool.shape[0], blk_size * kv_pool.shape[1], kv_pool.shape[2]
    )
    key_count = shard_piece.shape[1]
    page_ids = jnp.arange(key_count, dtype=jnp.int32) // PAGE
    page_used = jnp.any((row_pages[None, :] == page_ids[:, None]) & live_slots[None, :], axis=1)
    key_mask = jnp.broadcast_to(page_used[None, :], (own_rows, key_count))
    running_max, row_total, weighted = attend_block(
        softmax_state,
        query_heads,
        shard_piece[0].reshape(key_count, head_count, HD),
        shard_piece[1].reshape(key_count, head_count, HD),
        key_mask,
    )
    mixed = weighted / row_total[:, :, None]
    mixed = jnp.where((row_index < length)[None, :, None], mixed, 0.0)
    mixed = jnp.transpose(mixed, (1, 0, 2)).reshape(own_rows, head_width).astype(jnp.bfloat16)
    return (server_q, mixed)


def solution(mesh):
    in_specs = (
        P("dp", ("blk", "mp")),
        P(("mp", "blk"), "dp"),
        P(None, ("dp", "blk"), "mp"),
        P(None, ("dp", "blk"), "mp"),
        P(("dp", "blk"), None),
        P(("dp", "blk")),
        P(("dp", "blk")),
    )
    out_specs = (P("mp", "blk"), P(("dp", "blk"), "mp"))
    return jax.shard_map(body, mesh=mesh, in_specs=in_specs, out_specs=out_specs, check_vma=False)
```

```python
import jax
import jax.numpy as jnp
from jax import lax
from jax.sharding import PartitionSpec as P

HD = 224
PAGE = 16


def attend_block(softmax_state, query_heads, key_heads, value_heads, key_mask):
    running_max, row_total, weighted = softmax_state
    scores = jnp.einsum(
        "thd,khd->htk", query_heads, key_heads, preferred_element_type=jnp.float32
    ) * HD ** (-0.5)
    scores = jnp.where(key_mask[None], scores, -1e30)
    new_max = jnp.maximum(running_max, jnp.max(scores, axis=2))
    weights = jnp.where(key_mask[None], jnp.exp(scores - new_max[:, :, None]), 0.0)
    factor = jnp.exp(running_max - new_max)
    row_total = row_total * factor + jnp.sum(weights, axis=2)
    weighted = weighted * factor[:, :, None] + jnp.einsum(
        "htk,khd->htd",
        weights.astype(jnp.bfloat16),
        value_heads,
        preferred_element_type=jnp.float32,
    )
    return (new_max, row_total, weighted)


def body(tokens, trainer_q, kv_pool, prompt_kv, page_table, page_count, prompt_len):
    blk_size = lax.axis_size("blk")
    mp_size = lax.axis_size("mp")
    dp_size = lax.axis_size("dp")
    g = lax.axis_index("dp")
    b = lax.axis_index("blk")
    core = b % 2
    piece_rows, quarter_cols = trainer_q.shape
    trainer_rows = lax.all_gather(trainer_q.astype(jnp.bfloat16), "dp", axis=1, tiled=True)
    trainer_rows = trainer_rows.reshape(piece_rows, dp_size, quarter_cols)
    chosen = jnp.stack(
        [
            lax.dynamic_index_in_dim(trainer_rows, g, 1, keepdims=False),
            lax.dynamic_index_in_dim(trainer_rows, (g + 2) % dp_size, 1, keepdims=False),
        ]
    )
    chosen = lax.all_gather(chosen, "blk", axis=1, tiled=True)
    head_width = chosen.shape[1]
    half_rows = head_width // 2
    own_half = lax.dynamic_slice_in_dim(chosen[0], core * half_rows, half_rows, axis=0)
    from_next = lax.ppermute(own_half, "dp", [(i, (i - 1) % dp_size) for i in range(dp_size)])
    from_prev = lax.ppermute(own_half, "dp", [(i, (i + 1) % dp_size) for i in range(dp_size)])
    fetched = jnp.stack([from_next, from_prev])
    mate = lax.ppermute(fetched, "blk", [(i, i ^ 1) for i in range(blk_size)])
    first = jnp.where(core == 0, fetched, mate)
    second = jnp.where(core == 0, mate, fetched)
    whole = jnp.concatenate([first, second], axis=1)
    quarters = jnp.stack([chosen[0], whole[0], chosen[1], whole[1]])
    block_cols = quarter_cols * dp_size // blk_size
    blocks_per_quarter = quarter_cols // block_cols
    server_q = lax.dynamic_slice(
        quarters,
        ((b // blocks_per_quarter - g) % dp_size, 0, (b % blocks_per_quarter) * block_cols),
        (1, head_width, block_cols),
    )[0]
    group_rows, piece_cols = tokens.shape
    own_rows = group_rows // blk_size
    pieces = tokens.reshape(blk_size, 1, own_rows, piece_cols)
    pieces = jnp.broadcast_to(pieces, (blk_size, mp_size, own_rows, piece_cols))
    pieces = pieces.reshape(blk_size * mp_size, own_rows, piece_cols)
    pieces = lax.all_to_all(pieces, ("blk", "mp"), 0, 0, tiled=True)
    token_local = jnp.transpose(pieces, (1, 0, 2)).reshape(own_rows, -1)
    token_quarters = token_local.reshape(own_rows, dp_size, quarter_cols)
    token_quarters = jnp.concatenate([token_quarters, token_quarters], axis=1)
    token_quarters = lax.dynamic_slice_in_dim(token_quarters, g, dp_size, axis=1)
    queries = jnp.einsum(
        "tjd,jhd->th", token_quarters, quarters, preferred_element_type=jnp.float32
    )
    queries = queries.astype(jnp.bfloat16)
    head_count = head_width // HD
    query_heads = queries.reshape(own_rows, head_count, HD)
    length = prompt_len[0]
    row_pages = page_table[0]
    live_slots = jnp.arange(row_pages.shape[0], dtype=jnp.int32) < page_count[0]
    row_index = jnp.arange(own_rows, dtype=jnp.int32)
    own_mask = (row_index[None, :] <= row_index[:, None]) & (row_index[None, :] < length)
    softmax_state = (
        jnp.full((head_count, own_rows), -1e30, jnp.float32),
        jnp.zeros((head_count, own_rows), jnp.float32),
        jnp.zeros((head_count, own_rows, HD), jnp.float32),
    )
    softmax_state = attend_block(
        softmax_state,
        query_heads,
        prompt_kv[0].reshape(own_rows, head_count, HD),
        prompt_kv[1].reshape(own_rows, head_count, HD),
        own_mask,
    )
    shard_piece = lax.all_gather(kv_pool, "blk", axis=1, tiled=True)
    key_count = shard_piece.shape[1]
    page_ids = jnp.arange(key_count, dtype=jnp.int32) // PAGE
    page_used = jnp.any((row_pages[None, :] == page_ids[:, None]) & live_slots[None, :], axis=1)
    key_mask = jnp.broadcast_to(page_used[None, :], (own_rows, key_count))
    running_max, row_total, weighted = attend_block(
        softmax_state,
        query_heads,
        shard_piece[0].reshape(key_count, head_count, HD),
        shard_piece[1].reshape(key_count, head_count, HD),
        key_mask,
    )
    mixed = weighted / row_total[:, :, None]
    mixed = jnp.where((row_index < length)[None, :, None], mixed, 0.0)
    mixed = jnp.transpose(mixed, (1, 0, 2)).reshape(own_rows, head_width).astype(jnp.bfloat16)
    return (server_q, mixed)


def solution(mesh):
    in_specs = (
        P("dp", ("blk", "mp")),
        P(("mp", "blk"), "dp"),
        P(None, ("dp", "blk"), "mp"),
        P(None, ("dp", "blk"), "mp"),
        P(("dp", "blk"), None),
        P(("dp", "blk")),
        P(("dp", "blk")),
    )
    out_specs = (P("mp", "blk"), P(("dp", "blk"), "mp"))
    return jax.shard_map(body, mesh=mesh, in_specs=in_specs, out_specs=out_specs, check_vma=False)
```

```python
import jax
import jax.numpy as jnp
from jax import lax
from jax.sharding import PartitionSpec as P

HD = 224
PAGE = 16


def attend_block(softmax_state, query_heads, key_heads, value_heads, key_mask):
    running_max, row_total, weighted = softmax_state
    scores = jnp.einsum(
        "thd,khd->htk", query_heads, key_heads, preferred_element_type=jnp.float32
    ) * HD ** (-0.5)
    scores = jnp.where(key_mask[None], scores, -1e30)
    new_max = jnp.maximum(running_max, jnp.max(scores, axis=2))
    weights = jnp.where(key_mask[None], jnp.exp(scores - new_max[:, :, None]), 0.0)
    factor = jnp.exp(running_max - new_max)
    row_total = row_total * factor + jnp.sum(weights, axis=2)
    weighted = weighted * factor[:, :, None] + jnp.einsum(
        "htk,khd->htd",
        weights.astype(jnp.bfloat16),
        value_heads,
        preferred_element_type=jnp.float32,
    )
    return (new_max, row_total, weighted)


def body(tokens, trainer_q, kv_pool, prompt_kv, page_table, page_count, prompt_len):
    blk_size = lax.axis_size("blk")
    mp_size = lax.axis_size("mp")
    dp_size = lax.axis_size("dp")
    g = lax.axis_index("dp")
    b = lax.axis_index("blk")
    core = b % 2
    piece_rows, quarter_cols = trainer_q.shape
    trainer_rows = lax.all_gather(trainer_q.astype(jnp.bfloat16), "dp", axis=1, tiled=True)
    trainer_rows = trainer_rows.reshape(piece_rows, dp_size, quarter_cols)
    chosen = jnp.concatenate(
        [
            lax.dynamic_index_in_dim(trainer_rows, g, 1, keepdims=False),
            lax.dynamic_index_in_dim(trainer_rows, (g + 2) % dp_size, 1, keepdims=False),
        ],
        axis=1,
    )
    chosen = lax.all_gather(chosen, "blk", axis=0, tiled=True)
    chosen = (chosen[:, :quarter_cols], chosen[:, quarter_cols:])
    head_width = chosen[0].shape[0]
    half_rows = head_width // 2
    own_half = lax.dynamic_slice_in_dim(chosen[0], core * half_rows, half_rows, axis=0)
    from_next = lax.ppermute(own_half, "dp", [(i, (i - 1) % dp_size) for i in range(dp_size)])
    from_prev = lax.ppermute(own_half, "dp", [(i, (i + 1) % dp_size) for i in range(dp_size)])
    fetched = jnp.stack([from_next, from_prev])
    mate = lax.ppermute(fetched, "blk", [(i, i ^ 1) for i in range(blk_size)])
    first = jnp.where(core == 0, fetched, mate)
    second = jnp.where(core == 0, mate, fetched)
    whole = jnp.concatenate([first, second], axis=1)
    quarters = jnp.stack([chosen[0], whole[0], chosen[1], whole[1]])
    block_cols = quarter_cols * dp_size // blk_size
    blocks_per_quarter = quarter_cols // block_cols
    server_q = lax.dynamic_slice(
        quarters,
        ((b // blocks_per_quarter - g) % dp_size, 0, (b % blocks_per_quarter) * block_cols),
        (1, head_width, block_cols),
    )[0]
    group_rows, piece_cols = tokens.shape
    own_rows = group_rows // blk_size
    pieces = tokens.reshape(blk_size, 1, own_rows, piece_cols)
    pieces = jnp.broadcast_to(pieces, (blk_size, mp_size, own_rows, piece_cols))
    pieces = pieces.reshape(blk_size * mp_size, own_rows, piece_cols)
    pieces = lax.all_to_all(pieces, ("blk", "mp"), 0, 0, tiled=True)
    token_local = jnp.transpose(pieces, (1, 0, 2)).reshape(own_rows, -1)
    token_quarters = token_local.reshape(own_rows, dp_size, quarter_cols)
    token_quarters = jnp.concatenate([token_quarters, token_quarters], axis=1)
    token_quarters = lax.dynamic_slice_in_dim(token_quarters, g, dp_size, axis=1)
    queries = jnp.einsum(
        "tjd,jhd->th", token_quarters, quarters, preferred_element_type=jnp.float32
    )
    queries = queries.astype(jnp.bfloat16)
    head_count = head_width // HD
    query_heads = queries.reshape(own_rows, head_count, HD)
    length = prompt_len[0]
    row_pages = page_table[0]
    live_slots = jnp.arange(row_pages.shape[0], dtype=jnp.int32) < page_count[0]
    row_index = jnp.arange(own_rows, dtype=jnp.int32)
    own_mask = (row_index[None, :] <= row_index[:, None]) & (row_index[None, :] < length)
    softmax_state = (
        jnp.full((head_count, own_rows), -1e30, jnp.float32),
        jnp.zeros((head_count, own_rows), jnp.float32),
        jnp.zeros((head_count, own_rows, HD), jnp.float32),
    )
    softmax_state = attend_block(
        softmax_state,
        query_heads,
        prompt_kv[0].reshape(own_rows, head_count, HD),
        prompt_kv[1].reshape(own_rows, head_count, HD),
        own_mask,
    )
    shard_piece = lax.all_gather(kv_pool, "blk", axis=1, tiled=True)
    key_count = shard_piece.shape[1]
    page_ids = jnp.arange(key_count, dtype=jnp.int32) // PAGE
    page_used = jnp.any((row_pages[None, :] == page_ids[:, None]) & live_slots[None, :], axis=1)
    key_mask = jnp.broadcast_to(page_used[None, :], (own_rows, key_count))
    running_max, row_total, weighted = attend_block(
        softmax_state,
        query_heads,
        shard_piece[0].reshape(key_count, head_count, HD),
        shard_piece[1].reshape(key_count, head_count, HD),
        key_mask,
    )
    mixed = weighted / row_total[:, :, None]
    mixed = jnp.where((row_index < length)[None, :, None], mixed, 0.0)
    mixed = jnp.transpose(mixed, (1, 0, 2)).reshape(own_rows, head_width).astype(jnp.bfloat16)
    return (server_q, mixed)


def solution(mesh):
    in_specs = (
        P("dp", ("blk", "mp")),
        P(("mp", "blk"), "dp"),
        P(None, ("dp", "blk"), "mp"),
        P(None, ("dp", "blk"), "mp"),
        P(("dp", "blk"), None),
        P(("dp", "blk")),
        P(("dp", "blk")),
    )
    out_specs = (P("mp", "blk"), P(("dp", "blk"), "mp"))
    return jax.shard_map(body, mesh=mesh, in_specs=in_specs, out_specs=out_specs, check_vma=False)
```

```python
import jax
import jax.numpy as jnp
from jax import lax
from jax.sharding import PartitionSpec as P

HD = 224
PAGE = 16


def attend_block(softmax_state, query_heads, key_heads, value_heads, key_mask):
    running_max, row_total, weighted = softmax_state
    scores = jnp.einsum(
        "thd,khd->htk", query_heads, key_heads, preferred_element_type=jnp.float32
    ) * HD ** (-0.5)
    scores = jnp.where(key_mask[None], scores, -1e30)
    new_max = jnp.maximum(running_max, jnp.max(scores, axis=2))
    weights = jnp.where(key_mask[None], jnp.exp(scores - new_max[:, :, None]), 0.0)
    factor = jnp.exp(running_max - new_max)
    row_total = row_total * factor + jnp.sum(weights, axis=2)
    weighted = weighted * factor[:, :, None] + jnp.einsum(
        "htk,khd->htd",
        weights.astype(jnp.bfloat16),
        value_heads,
        preferred_element_type=jnp.float32,
    )
    return (new_max, row_total, weighted)


def body(tokens, trainer_q, kv_pool, prompt_kv, page_table, page_count, prompt_len):
    blk_size = lax.axis_size("blk")
    mp_size = lax.axis_size("mp")
    trainer_rows = lax.all_gather(trainer_q.astype(jnp.bfloat16), "dp", axis=1, tiled=True)
    head_weights = lax.all_gather(trainer_rows, "blk", axis=0, tiled=True)
    head_width, model_width = head_weights.shape
    block_cols = model_width // blk_size
    server_q = lax.dynamic_slice_in_dim(
        head_weights, lax.axis_index("blk") * block_cols, block_cols, axis=1
    )
    group_rows, piece_cols = tokens.shape
    own_rows = group_rows // blk_size
    pieces = tokens.reshape(blk_size, own_rows, piece_cols)
    pieces = lax.all_to_all(pieces, "blk", 0, 0, tiled=True)
    pieces = jnp.broadcast_to(pieces[None], (mp_size, blk_size, own_rows, piece_cols))
    pieces = lax.all_to_all(pieces, "mp", 0, 0, tiled=True)
    token_local = jnp.transpose(pieces, (2, 1, 0, 3)).reshape(own_rows, -1)
    queries = jnp.einsum(
        "td,hd->th", token_local, head_weights, preferred_element_type=jnp.float32
    )
    queries = queries.astype(jnp.bfloat16)
    head_count = head_width // HD
    query_heads = queries.reshape(own_rows, head_count, HD)
    length = prompt_len[0]
    row_pages = page_table[0]
    live_slots = jnp.arange(row_pages.shape[0], dtype=jnp.int32) < page_count[0]
    row_index = jnp.arange(own_rows, dtype=jnp.int32)
    own_mask = (row_index[None, :] <= row_index[:, None]) & (row_index[None, :] < length)
    softmax_state = (
        jnp.full((head_count, own_rows), -1e30, jnp.float32),
        jnp.zeros((head_count, own_rows), jnp.float32),
        jnp.zeros((head_count, own_rows, HD), jnp.float32),
    )
    softmax_state = attend_block(
        softmax_state,
        query_heads,
        prompt_kv[0].reshape(own_rows, head_count, HD),
        prompt_kv[1].reshape(own_rows, head_count, HD),
        own_mask,
    )
    shard_piece = lax.all_gather(kv_pool, "blk", axis=1, tiled=True)
    key_count = shard_piece.shape[1]
    page_ids = jnp.arange(key_count, dtype=jnp.int32) // PAGE
    page_used = jnp.any((row_pages[None, :] == page_ids[:, None]) & live_slots[None, :], axis=1)
    key_mask = jnp.broadcast_to(page_used[None, :], (own_rows, key_count))
    running_max, row_total, weighted = attend_block(
        softmax_state,
        query_heads,
        shard_piece[0].reshape(key_count, head_count, HD),
        shard_piece[1].reshape(key_count, head_count, HD),
        key_mask,
    )
    mixed = weighted / row_total[:, :, None]
    mixed = jnp.where((row_index < length)[None, :, None], mixed, 0.0)
    mixed = jnp.transpose(mixed, (1, 0, 2)).reshape(own_rows, head_width).astype(jnp.bfloat16)
    return (server_q, mixed)


def solution(mesh):
    in_specs = (
        P("dp", ("blk", "mp")),
        P(("mp", "blk"), "dp"),
        P(None, ("dp", "blk"), "mp"),
        P(None, ("dp", "blk"), "mp"),
        P(("dp", "blk"), None),
        P(("dp", "blk")),
        P(("dp", "blk")),
    )
    out_specs = (P("mp", "blk"), P(("dp", "blk"), "mp"))
    return jax.shard_map(body, mesh=mesh, in_specs=in_specs, out_specs=out_specs, check_vma=False)
```

```python
import jax
import jax.numpy as jnp
from jax import lax
from jax.experimental import pallas as pl
from jax.experimental.pallas import tpu as pltpu
from jax.sharding import PartitionSpec as P

HD = 224
PAGE = 16


def attend_block(softmax_state, query_heads, key_heads, value_heads, key_mask):
    running_max, row_total, weighted = softmax_state
    scores = jnp.einsum(
        "thd,khd->htk", query_heads, key_heads, preferred_element_type=jnp.float32
    ) * HD ** (-0.5)
    scores = jnp.where(key_mask[None], scores, -1e30)
    new_max = jnp.maximum(running_max, jnp.max(scores, axis=2))
    weights = jnp.where(key_mask[None], jnp.exp(scores - new_max[:, :, None]), 0.0)
    factor = jnp.exp(running_max - new_max)
    row_total = row_total * factor + jnp.sum(weights, axis=2)
    weighted = weighted * factor[:, :, None] + jnp.einsum(
        "htk,khd->htd",
        weights.astype(jnp.bfloat16),
        value_heads,
        preferred_element_type=jnp.float32,
    )
    return (new_max, row_total, weighted)


def dp_exchange_kernel(piece_ref, out_ref, local_sem, send_sems, recv_sems):
    n = lax.axis_size("dp")
    g = lax.axis_index("dp")
    b = lax.axis_index("blk")
    m = lax.axis_index("mp")
    barrier = pltpu.get_barrier_semaphore()
    for j in range(1, n):
        pl.semaphore_signal(
            barrier, inc=1, device_id=((g + j) % n, b, m), device_id_type=pl.DeviceIdType.MESH
        )
    pl.semaphore_wait(barrier, n - 1)
    local = pltpu.make_async_copy(piece_ref, out_ref.at[g], local_sem)
    local.start()
    sends = []
    for j in range(1, n):
        copy = pltpu.make_async_remote_copy(
            src_ref=piece_ref,
            dst_ref=out_ref.at[g],
            send_sem=send_sems.at[j - 1],
            recv_sem=recv_sems.at[j - 1],
            device_id=((g + j) % n, b, m),
            device_id_type=pl.DeviceIdType.MESH,
        )
        copy.start()
        sends.append(copy)
    local.wait()
    for copy in sends:
        copy.wait_send()
    for j in range(1, n):
        pltpu.make_async_remote_copy(
            src_ref=piece_ref,
            dst_ref=out_ref.at[(g - j) % n],
            send_sem=send_sems.at[j - 1],
            recv_sem=recv_sems.at[j - 1],
            device_id=((g - j) % n, b, m),
            device_id_type=pl.DeviceIdType.MESH,
        ).wait_recv()


def gather_dp(piece):
    n = lax.axis_size("dp")
    rows, cols = piece.shape
    out = pl.pallas_call(
        dp_exchange_kernel,
        out_shape=jax.ShapeDtypeStruct((n, rows, cols), piece.dtype),
        in_specs=[pl.BlockSpec(memory_space=pl.ANY)],
        out_specs=pl.BlockSpec(memory_space=pl.ANY),
        scratch_shapes=[
            pltpu.SemaphoreType.DMA(()),
            pltpu.SemaphoreType.DMA((n - 1,)),
            pltpu.SemaphoreType.DMA((n - 1,)),
        ],
        compiler_params=pltpu.CompilerParams(collective_id=0, has_side_effects=True),
    )(piece)
    return jnp.transpose(out, (1, 0, 2)).reshape(rows, n * cols)


def body(tokens, trainer_q, kv_pool, prompt_kv, page_table, page_count, prompt_len):
    blk_size = lax.axis_size("blk")
    mp_size = lax.axis_size("mp")
    trainer_rows = gather_dp(trainer_q.astype(jnp.bfloat16))
    head_weights = lax.all_gather(trainer_rows, "blk", axis=0, tiled=True)
    head_width, model_width = head_weights.shape
    block_cols = model_width // blk_size
    server_q = lax.dynamic_slice_in_dim(
        head_weights, lax.axis_index("blk") * block_cols, block_cols, axis=1
    )
    group_rows, piece_cols = tokens.shape
    own_rows = group_rows // blk_size
    pieces = tokens.reshape(blk_size, 1, own_rows, piece_cols)
    pieces = jnp.broadcast_to(pieces, (blk_size, mp_size, own_rows, piece_cols))
    pieces = pieces.reshape(blk_size * mp_size, own_rows, piece_cols)
    pieces = lax.all_to_all(pieces, ("blk", "mp"), 0, 0, tiled=True)
    token_local = jnp.transpose(pieces, (1, 0, 2)).reshape(own_rows, -1)
    queries = jnp.einsum(
        "td,hd->th", token_local, head_weights, preferred_element_type=jnp.float32
    )
    queries = queries.astype(jnp.bfloat16)
    head_count = head_width // HD
    query_heads = queries.reshape(own_rows, head_count, HD)
    length = prompt_len[0]
    row_pages = page_table[0]
    live_slots = jnp.arange(row_pages.shape[0], dtype=jnp.int32) < page_count[0]
    row_index = jnp.arange(own_rows, dtype=jnp.int32)
    own_mask = (row_index[None, :] <= row_index[:, None]) & (row_index[None, :] < length)
    softmax_state = (
        jnp.full((head_count, own_rows), -1e30, jnp.float32),
        jnp.zeros((head_count, own_rows), jnp.float32),
        jnp.zeros((head_count, own_rows, HD), jnp.float32),
    )
    softmax_state = attend_block(
        softmax_state,
        query_heads,
        prompt_kv[0].reshape(own_rows, head_count, HD),
        prompt_kv[1].reshape(own_rows, head_count, HD),
        own_mask,
    )
    shard_piece = lax.all_gather(kv_pool, "blk", axis=1, tiled=True)
    key_count = shard_piece.shape[1]
    page_ids = jnp.arange(key_count, dtype=jnp.int32) // PAGE
    page_used = jnp.any((row_pages[None, :] == page_ids[:, None]) & live_slots[None, :], axis=1)
    key_mask = jnp.broadcast_to(page_used[None, :], (own_rows, key_count))
    running_max, row_total, weighted = attend_block(
        softmax_state,
        query_heads,
        shard_piece[0].reshape(key_count, head_count, HD),
        shard_piece[1].reshape(key_count, head_count, HD),
        key_mask,
    )
    mixed = weighted / row_total[:, :, None]
    mixed = jnp.where((row_index < length)[None, :, None], mixed, 0.0)
    mixed = jnp.transpose(mixed, (1, 0, 2)).reshape(own_rows, head_width).astype(jnp.bfloat16)
    return (server_q, mixed)


def solution(mesh):
    in_specs = (
        P("dp", ("blk", "mp")),
        P(("mp", "blk"), "dp"),
        P(None, ("dp", "blk"), "mp"),
        P(None, ("dp", "blk"), "mp"),
        P(("dp", "blk"), None),
        P(("dp", "blk")),
        P(("dp", "blk")),
    )
    out_specs = (P("mp", "blk"), P(("dp", "blk"), "mp"))
    return jax.shard_map(body, mesh=mesh, in_specs=in_specs, out_specs=out_specs, check_vma=False)
```

```python
import jax
import jax.numpy as jnp
from jax import lax
from jax.experimental import pallas as pl
from jax.experimental.pallas import tpu as pltpu
from jax.sharding import PartitionSpec as P

HD = 224
PAGE = 16


def attend_block(softmax_state, query_heads, key_heads, value_heads, key_mask):
    running_max, row_total, weighted = softmax_state
    scores = jnp.einsum(
        "thd,khd->htk", query_heads, key_heads, preferred_element_type=jnp.float32
    ) * HD ** (-0.5)
    scores = jnp.where(key_mask[None], scores, -1e30)
    new_max = jnp.maximum(running_max, jnp.max(scores, axis=2))
    weights = jnp.where(key_mask[None], jnp.exp(scores - new_max[:, :, None]), 0.0)
    factor = jnp.exp(running_max - new_max)
    row_total = row_total * factor + jnp.sum(weights, axis=2)
    weighted = weighted * factor[:, :, None] + jnp.einsum(
        "htk,khd->htd",
        weights.astype(jnp.bfloat16),
        value_heads,
        preferred_element_type=jnp.float32,
    )
    return (new_max, row_total, weighted)


def dp_exchange_kernel(piece_ref, out_ref, local_sem, send_sems, recv_sems):
    n = lax.axis_size("dp")
    g = lax.axis_index("dp")
    b = lax.axis_index("blk")
    m = lax.axis_index("mp")
    barrier = pltpu.get_barrier_semaphore()
    for j in range(1, n):
        pl.semaphore_signal(
            barrier, inc=1, device_id=((g + j) % n, b, m), device_id_type=pl.DeviceIdType.MESH
        )
    pl.semaphore_wait(barrier, n - 1)
    local = pltpu.make_async_copy(piece_ref, out_ref.at[g], local_sem)
    local.start()
    sends = []
    for j in range(1, n):
        copy = pltpu.make_async_remote_copy(
            src_ref=piece_ref,
            dst_ref=out_ref.at[g],
            send_sem=send_sems.at[j - 1],
            recv_sem=recv_sems.at[j - 1],
            device_id=((g + j) % n, b, m),
            device_id_type=pl.DeviceIdType.MESH,
        )
        copy.start()
        sends.append(copy)
    local.wait()
    for copy in sends:
        copy.wait_send()
    for j in range(1, n):
        pltpu.make_async_remote_copy(
            src_ref=piece_ref,
            dst_ref=out_ref.at[(g - j) % n],
            send_sem=send_sems.at[j - 1],
            recv_sem=recv_sems.at[j - 1],
            device_id=((g - j) % n, b, m),
            device_id_type=pl.DeviceIdType.MESH,
        ).wait_recv()


def gather_dp(piece):
    n = lax.axis_size("dp")
    rows, cols = piece.shape
    out = pl.pallas_call(
        dp_exchange_kernel,
        out_shape=jax.ShapeDtypeStruct((n, rows, cols), piece.dtype),
        in_specs=[pl.BlockSpec(memory_space=pl.ANY)],
        out_specs=pl.BlockSpec(memory_space=pl.ANY),
        scratch_shapes=[
            pltpu.SemaphoreType.DMA(()),
            pltpu.SemaphoreType.DMA((n - 1,)),
            pltpu.SemaphoreType.DMA((n - 1,)),
        ],
        compiler_params=pltpu.CompilerParams(collective_id=0, has_side_effects=True),
    )(piece)
    return jnp.transpose(out, (1, 0, 2)).reshape(rows, n * cols)


def body(tokens, trainer_q, kv_pool, prompt_kv, page_table, page_count, prompt_len):
    blk_size = lax.axis_size("blk")
    mp_size = lax.axis_size("mp")
    trainer_rows = gather_dp(trainer_q.astype(jnp.bfloat16))
    head_weights = lax.all_gather(trainer_rows, "blk", axis=0, tiled=True)
    head_width, model_width = head_weights.shape
    block_cols = model_width // blk_size
    server_q = lax.dynamic_slice_in_dim(
        head_weights, lax.axis_index("blk") * block_cols, block_cols, axis=1
    )
    shard_piece = lax.all_gather(kv_pool, "blk", axis=1, tiled=True)
    tokens, shard_piece = lax.optimization_barrier((tokens, shard_piece))
    group_rows, piece_cols = tokens.shape
    own_rows = group_rows // blk_size
    pieces = tokens.reshape(blk_size, 1, own_rows, piece_cols)
    pieces = jnp.broadcast_to(pieces, (blk_size, mp_size, own_rows, piece_cols))
    pieces = pieces.reshape(blk_size * mp_size, own_rows, piece_cols)
    pieces = lax.all_to_all(pieces, ("blk", "mp"), 0, 0, tiled=True)
    token_local = jnp.transpose(pieces, (1, 0, 2)).reshape(own_rows, -1)
    queries = jnp.einsum(
        "td,hd->th", token_local, head_weights, preferred_element_type=jnp.float32
    )
    queries = queries.astype(jnp.bfloat16)
    head_count = head_width // HD
    query_heads = queries.reshape(own_rows, head_count, HD)
    length = prompt_len[0]
    row_pages = page_table[0]
    live_slots = jnp.arange(row_pages.shape[0], dtype=jnp.int32) < page_count[0]
    row_index = jnp.arange(own_rows, dtype=jnp.int32)
    own_mask = (row_index[None, :] <= row_index[:, None]) & (row_index[None, :] < length)
    softmax_state = (
        jnp.full((head_count, own_rows), -1e30, jnp.float32),
        jnp.zeros((head_count, own_rows), jnp.float32),
        jnp.zeros((head_count, own_rows, HD), jnp.float32),
    )
    softmax_state = attend_block(
        softmax_state,
        query_heads,
        prompt_kv[0].reshape(own_rows, head_count, HD),
        prompt_kv[1].reshape(own_rows, head_count, HD),
        own_mask,
    )
    key_count = shard_piece.shape[1]
    page_ids = jnp.arange(key_count, dtype=jnp.int32) // PAGE
    page_used = jnp.any((row_pages[None, :] == page_ids[:, None]) & live_slots[None, :], axis=1)
    key_mask = jnp.broadcast_to(page_used[None, :], (own_rows, key_count))
    running_max, row_total, weighted = attend_block(
        softmax_state,
        query_heads,
        shard_piece[0].reshape(key_count, head_count, HD),
        shard_piece[1].reshape(key_count, head_count, HD),
        key_mask,
    )
    mixed = weighted / row_total[:, :, None]
    mixed = jnp.where((row_index < length)[None, :, None], mixed, 0.0)
    mixed = jnp.transpose(mixed, (1, 0, 2)).reshape(own_rows, head_width).astype(jnp.bfloat16)
    return (server_q, mixed)


def solution(mesh):
    in_specs = (
        P("dp", ("blk", "mp")),
        P(("mp", "blk"), "dp"),
        P(None, ("dp", "blk"), "mp"),
        P(None, ("dp", "blk"), "mp"),
        P(("dp", "blk"), None),
        P(("dp", "blk")),
        P(("dp", "blk")),
    )
    out_specs = (P("mp", "blk"), P(("dp", "blk"), "mp"))
    return jax.shard_map(body, mesh=mesh, in_specs=in_specs, out_specs=out_specs, check_vma=False)
```

```python
import jax
import jax.numpy as jnp
from jax import lax
from jax.experimental import pallas as pl
from jax.experimental.pallas import tpu as pltpu
from jax.sharding import PartitionSpec as P

HD = 224
PAGE = 16


def attend_block(softmax_state, query_heads, key_heads, value_heads, key_mask):
    running_max, row_total, weighted = softmax_state
    scores = jnp.einsum(
        "thd,khd->htk", query_heads, key_heads, preferred_element_type=jnp.float32
    ) * HD ** (-0.5)
    scores = jnp.where(key_mask[None], scores, -1e30)
    new_max = jnp.maximum(running_max, jnp.max(scores, axis=2))
    weights = jnp.where(key_mask[None], jnp.exp(scores - new_max[:, :, None]), 0.0)
    factor = jnp.exp(running_max - new_max)
    row_total = row_total * factor + jnp.sum(weights, axis=2)
    weighted = weighted * factor[:, :, None] + jnp.einsum(
        "htk,khd->htd",
        weights.astype(jnp.bfloat16),
        value_heads,
        preferred_element_type=jnp.float32,
    )
    return (new_max, row_total, weighted)


def dp_exchange_kernel(piece_ref, out_ref, local_sem, send_sems, recv_sems):
    n = lax.axis_size("dp")
    g = lax.axis_index("dp")
    b = lax.axis_index("blk")
    m = lax.axis_index("mp")
    barrier = pltpu.get_barrier_semaphore()
    for j in range(1, n):
        pl.semaphore_signal(
            barrier, inc=1, device_id=((g + j) % n, b, m), device_id_type=pl.DeviceIdType.MESH
        )
    pl.semaphore_wait(barrier, n - 1)
    local = pltpu.make_async_copy(piece_ref, out_ref.at[g], local_sem)
    local.start()
    sends = []
    for j in range(1, n):
        copy = pltpu.make_async_remote_copy(
            src_ref=piece_ref,
            dst_ref=out_ref.at[g],
            send_sem=send_sems.at[j - 1],
            recv_sem=recv_sems.at[j - 1],
            device_id=((g + j) % n, b, m),
            device_id_type=pl.DeviceIdType.MESH,
        )
        copy.start()
        sends.append(copy)
    local.wait()
    for copy in sends:
        copy.wait_send()
    for j in range(1, n):
        pltpu.make_async_remote_copy(
            src_ref=piece_ref,
            dst_ref=out_ref.at[(g - j) % n],
            send_sem=send_sems.at[j - 1],
            recv_sem=recv_sems.at[j - 1],
            device_id=((g - j) % n, b, m),
            device_id_type=pl.DeviceIdType.MESH,
        ).wait_recv()


def gather_dp(piece):
    n = lax.axis_size("dp")
    rows, cols = piece.shape
    out = pl.pallas_call(
        dp_exchange_kernel,
        out_shape=jax.ShapeDtypeStruct((n, rows, cols), piece.dtype),
        in_specs=[pl.BlockSpec(memory_space=pl.ANY)],
        out_specs=pl.BlockSpec(memory_space=pl.ANY),
        scratch_shapes=[
            pltpu.SemaphoreType.DMA(()),
            pltpu.SemaphoreType.DMA((n - 1,)),
            pltpu.SemaphoreType.DMA((n - 1,)),
        ],
        compiler_params=pltpu.CompilerParams(collective_id=0, has_side_effects=True),
    )(piece)
    return jnp.transpose(out, (1, 0, 2)).reshape(rows, n * cols)


def body(tokens, trainer_q, kv_pool, prompt_kv, page_table, page_count, prompt_len):
    blk_size = lax.axis_size("blk")
    mp_size = lax.axis_size("mp")
    trainer_rows = gather_dp(trainer_q.astype(jnp.bfloat16))
    half_cols = trainer_rows.shape[1] // 2
    weight_halves = [
        lax.all_gather(trainer_rows[:, :half_cols], "blk", axis=0, tiled=True),
        lax.all_gather(trainer_rows[:, half_cols:], "blk", axis=0, tiled=True),
    ]
    head_width, model_width = weight_halves[0].shape[0], trainer_rows.shape[1]
    block_cols = model_width // blk_size
    b = lax.axis_index("blk")
    halves_per_blocks = blk_size // 2
    server_q = jnp.where(
        b < halves_per_blocks,
        lax.dynamic_slice_in_dim(
            weight_halves[0], (b % halves_per_blocks) * block_cols, block_cols, axis=1
        ),
        lax.dynamic_slice_in_dim(
            weight_halves[1], (b % halves_per_blocks) * block_cols, block_cols, axis=1
        ),
    )
    group_rows, piece_cols = tokens.shape
    own_rows = group_rows // blk_size
    pieces = tokens.reshape(blk_size, 1, own_rows, piece_cols)
    pieces = jnp.broadcast_to(pieces, (blk_size, mp_size, own_rows, piece_cols))
    pieces = pieces.reshape(blk_size * mp_size, own_rows, piece_cols)
    pieces = lax.all_to_all(pieces, ("blk", "mp"), 0, 0, tiled=True)
    token_local = jnp.transpose(pieces, (1, 0, 2)).reshape(own_rows, -1)
    queries = jnp.einsum(
        "td,hd->th", token_local[:, :half_cols], weight_halves[0], preferred_element_type=jnp.float32
    ) + jnp.einsum(
        "td,hd->th", token_local[:, half_cols:], weight_halves[1], preferred_element_type=jnp.float32
    )
    queries = queries.astype(jnp.bfloat16)
    head_count = head_width // HD
    query_heads = queries.reshape(own_rows, head_count, HD)
    length = prompt_len[0]
    row_pages = page_table[0]
    live_slots = jnp.arange(row_pages.shape[0], dtype=jnp.int32) < page_count[0]
    row_index = jnp.arange(own_rows, dtype=jnp.int32)
    own_mask = (row_index[None, :] <= row_index[:, None]) & (row_index[None, :] < length)
    softmax_state = (
        jnp.full((head_count, own_rows), -1e30, jnp.float32),
        jnp.zeros((head_count, own_rows), jnp.float32),
        jnp.zeros((head_count, own_rows, HD), jnp.float32),
    )
    softmax_state = attend_block(
        softmax_state,
        query_heads,
        prompt_kv[0].reshape(own_rows, head_count, HD),
        prompt_kv[1].reshape(own_rows, head_count, HD),
        own_mask,
    )
    shard_piece = lax.all_gather(kv_pool, "blk", axis=1, tiled=True)
    key_count = shard_piece.shape[1]
    page_ids = jnp.arange(key_count, dtype=jnp.int32) // PAGE
    page_used = jnp.any((row_pages[None, :] == page_ids[:, None]) & live_slots[None, :], axis=1)
    key_mask = jnp.broadcast_to(page_used[None, :], (own_rows, key_count))
    running_max, row_total, weighted = attend_block(
        softmax_state,
        query_heads,
        shard_piece[0].reshape(key_count, head_count, HD),
        shard_piece[1].reshape(key_count, head_count, HD),
        key_mask,
    )
    mixed = weighted / row_total[:, :, None]
    mixed = jnp.where((row_index < length)[None, :, None], mixed, 0.0)
    mixed = jnp.transpose(mixed, (1, 0, 2)).reshape(own_rows, head_width).astype(jnp.bfloat16)
    return (server_q, mixed)


def solution(mesh):
    in_specs = (
        P("dp", ("blk", "mp")),
        P(("mp", "blk"), "dp"),
        P(None, ("dp", "blk"), "mp"),
        P(None, ("dp", "blk"), "mp"),
        P(("dp", "blk"), None),
        P(("dp", "blk")),
        P(("dp", "blk")),
    )
    out_specs = (P("mp", "blk"), P(("dp", "blk"), "mp"))
    return jax.shard_map(body, mesh=mesh, in_specs=in_specs, out_specs=out_specs, check_vma=False)
```

```python
import jax
import jax.numpy as jnp
from jax import lax
from jax.sharding import PartitionSpec as P

HD = 224
PAGE = 16


def attend_block(softmax_state, query_heads, key_heads, value_heads, key_mask):
    running_max, row_total, weighted = softmax_state
    scores = jnp.einsum(
        "thd,khd->htk", query_heads, key_heads, preferred_element_type=jnp.float32
    ) * HD ** (-0.5)
    scores = jnp.where(key_mask[None], scores, -1e30)
    new_max = jnp.maximum(running_max, jnp.max(scores, axis=2))
    weights = jnp.where(key_mask[None], jnp.exp(scores - new_max[:, :, None]), 0.0)
    factor = jnp.exp(running_max - new_max)
    row_total = row_total * factor + jnp.sum(weights, axis=2)
    weighted = weighted * factor[:, :, None] + jnp.einsum(
        "htk,khd->htd",
        weights.astype(jnp.bfloat16),
        value_heads,
        preferred_element_type=jnp.float32,
    )
    return (new_max, row_total, weighted)


def body(tokens, trainer_q, kv_pool, prompt_kv, page_table, page_count, prompt_len):
    blk_size = lax.axis_size("blk")
    mp_size = lax.axis_size("mp")
    dp_size = lax.axis_size("dp")
    g = lax.axis_index("dp")
    b = lax.axis_index("blk")
    core = b % 2
    piece_rows, quarter_cols = trainer_q.shape
    trainer_rows = lax.all_gather(trainer_q.astype(jnp.bfloat16), "dp", axis=1, tiled=True)
    trainer_rows = trainer_rows.reshape(piece_rows, dp_size, quarter_cols)
    shard_piece = lax.all_gather(kv_pool, "blk", axis=1, tiled=True)
    own_piece = lax.dynamic_index_in_dim(trainer_rows, g, 1, keepdims=False)
    far_piece = lax.dynamic_index_in_dim(trainer_rows, (g + 2) % dp_size, 1, keepdims=False)
    own_piece, shard_piece = lax.optimization_barrier((own_piece, shard_piece))
    own_quarter = lax.all_gather(own_piece, "blk", axis=0, tiled=True)
    far_piece, own_quarter = lax.optimization_barrier((far_piece, own_quarter))
    far_quarter = lax.all_gather(far_piece, "blk", axis=0, tiled=True)
    chosen = (own_quarter, far_quarter)
    head_width = own_quarter.shape[0]
    half_rows = head_width // 2
    own_half = lax.dynamic_slice_in_dim(own_quarter, core * half_rows, half_rows, axis=0)
    from_next = lax.ppermute(own_half, "dp", [(i, (i - 1) % dp_size) for i in range(dp_size)])
    from_prev = lax.ppermute(own_half, "dp", [(i, (i + 1) % dp_size) for i in range(dp_size)])
    fetched = jnp.stack([from_next, from_prev])
    mate = lax.ppermute(fetched, "blk", [(i, i ^ 1) for i in range(blk_size)])
    first = jnp.where(core == 0, fetched, mate)
    second = jnp.where(core == 0, mate, fetched)
    whole = jnp.concatenate([first, second], axis=1)
    quarters = jnp.stack([chosen[0], whole[0], chosen[1], whole[1]])
    block_cols = quarter_cols * dp_size // blk_size
    blocks_per_quarter = quarter_cols // block_cols
    server_q = lax.dynamic_slice(
        quarters,
        ((b // blocks_per_quarter - g) % dp_size, 0, (b % blocks_per_quarter) * block_cols),
        (1, head_width, block_cols),
    )[0]
    group_rows, piece_cols = tokens.shape
    own_rows = group_rows // blk_size
    pieces = tokens.reshape(blk_size, 1, own_rows, piece_cols)
    pieces = jnp.broadcast_to(pieces, (blk_size, mp_size, own_rows, piece_cols))
    pieces = pieces.reshape(blk_size * mp_size, own_rows, piece_cols)
    pieces = lax.all_to_all(pieces, ("blk", "mp"), 0, 0, tiled=True)
    token_local = jnp.transpose(pieces, (1, 0, 2)).reshape(own_rows, -1)
    token_quarters = token_local.reshape(own_rows, dp_size, quarter_cols)
    token_quarters = jnp.concatenate([token_quarters, token_quarters], axis=1)
    token_quarters = lax.dynamic_slice_in_dim(token_quarters, g, dp_size, axis=1)
    queries = jnp.einsum(
        "tjd,jhd->th", token_quarters, quarters, preferred_element_type=jnp.float32
    )
    queries = queries.astype(jnp.bfloat16)
    head_count = head_width // HD
    query_heads = queries.reshape(own_rows, head_count, HD)
    length = prompt_len[0]
    row_pages = page_table[0]
    live_slots = jnp.arange(row_pages.shape[0], dtype=jnp.int32) < page_count[0]
    row_index = jnp.arange(own_rows, dtype=jnp.int32)
    own_mask = (row_index[None, :] <= row_index[:, None]) & (row_index[None, :] < length)
    softmax_state = (
        jnp.full((head_count, own_rows), -1e30, jnp.float32),
        jnp.zeros((head_count, own_rows), jnp.float32),
        jnp.zeros((head_count, own_rows, HD), jnp.float32),
    )
    softmax_state = attend_block(
        softmax_state,
        query_heads,
        prompt_kv[0].reshape(own_rows, head_count, HD),
        prompt_kv[1].reshape(own_rows, head_count, HD),
        own_mask,
    )
    key_count = shard_piece.shape[1]
    page_ids = jnp.arange(key_count, dtype=jnp.int32) // PAGE
    page_used = jnp.any((row_pages[None, :] == page_ids[:, None]) & live_slots[None, :], axis=1)
    key_mask = jnp.broadcast_to(page_used[None, :], (own_rows, key_count))
    running_max, row_total, weighted = attend_block(
        softmax_state,
        query_heads,
        shard_piece[0].reshape(key_count, head_count, HD),
        shard_piece[1].reshape(key_count, head_count, HD),
        key_mask,
    )
    mixed = weighted / row_total[:, :, None]
    mixed = jnp.where((row_index < length)[None, :, None], mixed, 0.0)
    mixed = jnp.transpose(mixed, (1, 0, 2)).reshape(own_rows, head_width).astype(jnp.bfloat16)
    return (server_q, mixed)


def solution(mesh):
    in_specs = (
        P("dp", ("blk", "mp")),
        P(("mp", "blk"), "dp"),
        P(None, ("dp", "blk"), "mp"),
        P(None, ("dp", "blk"), "mp"),
        P(("dp", "blk"), None),
        P(("dp", "blk")),
        P(("dp", "blk")),
    )
    out_specs = (P("mp", "blk"), P(("dp", "blk"), "mp"))
    return jax.shard_map(body, mesh=mesh, in_specs=in_specs, out_specs=out_specs, check_vma=False)
```

```python
import jax
import jax.numpy as jnp
from jax import lax
from jax.experimental import pallas as pl
from jax.experimental.pallas import tpu as pltpu
from jax.sharding import PartitionSpec as P

HD = 224
PAGE = 16


def attend_block(softmax_state, query_heads, key_heads, value_heads, key_mask):
    running_max, row_total, weighted = softmax_state
    scores = jnp.einsum(
        "thd,khd->htk", query_heads, key_heads, preferred_element_type=jnp.float32
    ) * HD ** (-0.5)
    scores = jnp.where(key_mask[None], scores, -1e30)
    new_max = jnp.maximum(running_max, jnp.max(scores, axis=2))
    weights = jnp.where(key_mask[None], jnp.exp(scores - new_max[:, :, None]), 0.0)
    factor = jnp.exp(running_max - new_max)
    row_total = row_total * factor + jnp.sum(weights, axis=2)
    weighted = weighted * factor[:, :, None] + jnp.einsum(
        "htk,khd->htd",
        weights.astype(jnp.bfloat16),
        value_heads,
        preferred_element_type=jnp.float32,
    )
    return (new_max, row_total, weighted)


def mate_swap_kernel(x_ref, out_ref, send_sem, recv_sem):
    g = lax.axis_index("dp")
    b = lax.axis_index("blk")
    m = lax.axis_index("mp")
    mate = b + 1 - 2 * (b % 2)
    barrier = pltpu.get_barrier_semaphore()
    pl.semaphore_signal(barrier, inc=1, device_id=(g, mate, m), device_id_type=pl.DeviceIdType.MESH)
    pl.semaphore_wait(barrier, 1)
    copy = pltpu.make_async_remote_copy(
        src_ref=x_ref,
        dst_ref=out_ref,
        send_sem=send_sem,
        recv_sem=recv_sem,
        device_id=(g, mate, m),
        device_id_type=pl.DeviceIdType.MESH,
    )
    copy.start()
    copy.wait()


def swap_with_mate(x):
    return pl.pallas_call(
        mate_swap_kernel,
        out_shape=jax.ShapeDtypeStruct(x.shape, x.dtype),
        in_specs=[pl.BlockSpec(memory_space=pl.ANY)],
        out_specs=pl.BlockSpec(memory_space=pl.ANY),
        scratch_shapes=[pltpu.SemaphoreType.DMA(()), pltpu.SemaphoreType.DMA(())],
        compiler_params=pltpu.CompilerParams(collective_id=0, has_side_effects=True),
    )(x)


def body(tokens, trainer_q, kv_pool, prompt_kv, page_table, page_count, prompt_len):
    blk_size = lax.axis_size("blk")
    mp_size = lax.axis_size("mp")
    dp_size = lax.axis_size("dp")
    g = lax.axis_index("dp")
    b = lax.axis_index("blk")
    core = b % 2
    piece_rows, quarter_cols = trainer_q.shape
    trainer_rows = lax.all_gather(trainer_q.astype(jnp.bfloat16), "dp", axis=1, tiled=True)
    trainer_rows = trainer_rows.reshape(piece_rows, dp_size, quarter_cols)
    shard_piece = lax.all_gather(kv_pool, "blk", axis=1, tiled=True)
    own_piece = lax.dynamic_index_in_dim(trainer_rows, g, 1, keepdims=False)
    far_piece = lax.dynamic_index_in_dim(trainer_rows, (g + 2) % dp_size, 1, keepdims=False)
    group_rows, piece_cols = tokens.shape
    own_rows = group_rows // blk_size
    pieces = tokens.reshape(blk_size, 1, own_rows, piece_cols)
    pieces = jnp.broadcast_to(pieces, (blk_size, mp_size, own_rows, piece_cols))
    pieces = pieces.reshape(blk_size * mp_size, own_rows, piece_cols)
    pieces = lax.all_to_all(pieces, ("blk", "mp"), 0, 0, tiled=True)
    own_piece, shard_piece, pieces = lax.optimization_barrier((own_piece, shard_piece, pieces))
    own_quarter = lax.all_gather(own_piece, "blk", axis=0, tiled=True)
    far_piece, own_quarter = lax.optimization_barrier((far_piece, own_quarter))
    far_quarter = lax.all_gather(far_piece, "blk", axis=0, tiled=True)
    chosen = (own_quarter, far_quarter)
    head_width = own_quarter.shape[0]
    half_rows = head_width // 2
    own_half = lax.dynamic_slice_in_dim(own_quarter, core * half_rows, half_rows, axis=0)
    from_next = lax.ppermute(own_half, "dp", [(i, (i - 1) % dp_size) for i in range(dp_size)])
    from_prev = lax.ppermute(own_half, "dp", [(i, (i + 1) % dp_size) for i in range(dp_size)])
    fetched = jnp.stack([from_next, from_prev])
    mate = swap_with_mate(fetched)
    first = jnp.where(core == 0, fetched, mate)
    second = jnp.where(core == 0, mate, fetched)
    whole = jnp.concatenate([first, second], axis=1)
    quarters = jnp.stack([chosen[0], whole[0], chosen[1], whole[1]])
    block_cols = quarter_cols * dp_size // blk_size
    blocks_per_quarter = quarter_cols // block_cols
    server_q = lax.dynamic_slice(
        quarters,
        ((b // blocks_per_quarter - g) % dp_size, 0, (b % blocks_per_quarter) * block_cols),
        (1, head_width, block_cols),
    )[0]
    token_local = jnp.transpose(pieces, (1, 0, 2)).reshape(own_rows, -1)
    token_quarters = token_local.reshape(own_rows, dp_size, quarter_cols)
    token_quarters = jnp.concatenate([token_quarters, token_quarters], axis=1)
    token_quarters = lax.dynamic_slice_in_dim(token_quarters, g, dp_size, axis=1)
    queries = jnp.einsum(
        "tjd,jhd->th", token_quarters, quarters, preferred_element_type=jnp.float32
    )
    queries = queries.astype(jnp.bfloat16)
    head_count = head_width // HD
    query_heads = queries.reshape(own_rows, head_count, HD)
    length = prompt_len[0]
    row_pages = page_table[0]
    live_slots = jnp.arange(row_pages.shape[0], dtype=jnp.int32) < page_count[0]
    row_index = jnp.arange(own_rows, dtype=jnp.int32)
    own_mask = (row_index[None, :] <= row_index[:, None]) & (row_index[None, :] < length)
    softmax_state = (
        jnp.full((head_count, own_rows), -1e30, jnp.float32),
        jnp.zeros((head_count, own_rows), jnp.float32),
        jnp.zeros((head_count, own_rows, HD), jnp.float32),
    )
    softmax_state = attend_block(
        softmax_state,
        query_heads,
        prompt_kv[0].reshape(own_rows, head_count, HD),
        prompt_kv[1].reshape(own_rows, head_count, HD),
        own_mask,
    )
    key_count = shard_piece.shape[1]
    page_ids = jnp.arange(key_count, dtype=jnp.int32) // PAGE
    page_used = jnp.any((row_pages[None, :] == page_ids[:, None]) & live_slots[None, :], axis=1)
    key_mask = jnp.broadcast_to(page_used[None, :], (own_rows, key_count))
    running_max, row_total, weighted = attend_block(
        softmax_state,
        query_heads,
        shard_piece[0].reshape(key_count, head_count, HD),
        shard_piece[1].reshape(key_count, head_count, HD),
        key_mask,
    )
    mixed = weighted / row_total[:, :, None]
    mixed = jnp.where((row_index < length)[None, :, None], mixed, 0.0)
    mixed = jnp.transpose(mixed, (1, 0, 2)).reshape(own_rows, head_width).astype(jnp.bfloat16)
    return (server_q, mixed)


def solution(mesh):
    in_specs = (
        P("dp", ("blk", "mp")),
        P(("mp", "blk"), "dp"),
        P(None, ("dp", "blk"), "mp"),
        P(None, ("dp", "blk"), "mp"),
        P(("dp", "blk"), None),
        P(("dp", "blk")),
        P(("dp", "blk")),
    )
    out_specs = (P("mp", "blk"), P(("dp", "blk"), "mp"))
    return jax.shard_map(body, mesh=mesh, in_specs=in_specs, out_specs=out_specs, check_vma=False)
```

```python
import jax
import jax.numpy as jnp
from jax import lax
from jax.experimental import pallas as pl
from jax.experimental.pallas import tpu as pltpu
from jax.sharding import PartitionSpec as P

HD = 224
PAGE = 16


def attend_block(softmax_state, query_heads, key_heads, value_heads, key_mask):
    running_max, row_total, weighted = softmax_state
    scores = jnp.einsum(
        "thd,khd->htk", query_heads, key_heads, preferred_element_type=jnp.float32
    ) * HD ** (-0.5)
    scores = jnp.where(key_mask[None], scores, -1e30)
    new_max = jnp.maximum(running_max, jnp.max(scores, axis=2))
    weights = jnp.where(key_mask[None], jnp.exp(scores - new_max[:, :, None]), 0.0)
    factor = jnp.exp(running_max - new_max)
    row_total = row_total * factor + jnp.sum(weights, axis=2)
    weighted = weighted * factor[:, :, None] + jnp.einsum(
        "htk,khd->htd",
        weights.astype(jnp.bfloat16),
        value_heads,
        preferred_element_type=jnp.float32,
    )
    return (new_max, row_total, weighted)


def kv_gather_kernel(piece_ref, out_ref, local_sem, send_sems, recv_sems, fwd_send, fwd_recv):
    chips = lax.axis_size("blk") // 2
    g = lax.axis_index("dp")
    b = lax.axis_index("blk")
    m = lax.axis_index("mp")
    c = b // 2
    k = b % 2
    mate = 2 * c + 1 - k

    def peer(j):
        return (g, 2 * ((c + j) % chips) + k, m)

    def source(j):
        return 2 * ((c + chips - j) % chips) + k

    def mate_slot(j):
        return 2 * ((c + chips - j) % chips) + 1 - k

    barrier = pltpu.get_barrier_semaphore()
    for j in range(1, chips):
        pl.semaphore_signal(barrier, inc=1, device_id=peer(j), device_id_type=pl.DeviceIdType.MESH)
    pl.semaphore_signal(barrier, inc=1, device_id=(g, mate, m), device_id_type=pl.DeviceIdType.MESH)
    pl.semaphore_wait(barrier, chips)
    local = pltpu.make_async_copy(piece_ref, out_ref.at[b], local_sem)
    local.start()
    sends = []
    for j in range(1, chips):
        copy = pltpu.make_async_remote_copy(
            src_ref=piece_ref, dst_ref=out_ref.at[b], send_sem=send_sems.at[j],
            recv_sem=recv_sems.at[j], device_id=peer(j), device_id_type=pl.DeviceIdType.MESH,
        )
        copy.start()
        sends.append(copy)
    to_mate = pltpu.make_async_remote_copy(
        src_ref=piece_ref, dst_ref=out_ref.at[b], send_sem=send_sems.at[0],
        recv_sem=recv_sems.at[0], device_id=(g, mate, m), device_id_type=pl.DeviceIdType.MESH,
    )
    to_mate.start()
    forwards = []
    for j in range(1, chips):
        pltpu.make_async_remote_copy(
            src_ref=piece_ref, dst_ref=out_ref.at[source(j)], send_sem=send_sems.at[j],
            recv_sem=recv_sems.at[j], device_id=peer(j), device_id_type=pl.DeviceIdType.MESH,
        ).wait_recv()
        copy = pltpu.make_async_remote_copy(
            src_ref=out_ref.at[source(j)], dst_ref=out_ref.at[source(j)], send_sem=fwd_send.at[j],
            recv_sem=fwd_recv.at[j], device_id=(g, mate, m), device_id_type=pl.DeviceIdType.MESH,
        )
        copy.start()
        forwards.append(copy)
    local.wait()
    for copy in sends:
        copy.wait_send()
    to_mate.wait_send()
    pltpu.make_async_remote_copy(
        src_ref=piece_ref, dst_ref=out_ref.at[mate], send_sem=send_sems.at[0],
        recv_sem=recv_sems.at[0], device_id=(g, mate, m), device_id_type=pl.DeviceIdType.MESH,
    ).wait_recv()
    for copy in forwards:
        copy.wait_send()
    for j in range(1, chips):
        pltpu.make_async_remote_copy(
            src_ref=out_ref.at[mate_slot(j)], dst_ref=out_ref.at[mate_slot(j)], send_sem=fwd_send.at[j],
            recv_sem=fwd_recv.at[j], device_id=(g, mate, m), device_id_type=pl.DeviceIdType.MESH,
        ).wait_recv()


def gather_kv(piece):
    n = lax.axis_size("blk")
    chips = n // 2
    out = pl.pallas_call(
        kv_gather_kernel,
        out_shape=jax.ShapeDtypeStruct((n,) + piece.shape, piece.dtype),
        in_specs=[pl.BlockSpec(memory_space=pl.ANY)],
        out_specs=pl.BlockSpec(memory_space=pl.ANY),
        scratch_shapes=[
            pltpu.SemaphoreType.DMA(()),
            pltpu.SemaphoreType.DMA((chips,)),
            pltpu.SemaphoreType.DMA((chips,)),
            pltpu.SemaphoreType.DMA((chips,)),
            pltpu.SemaphoreType.DMA((chips,)),
        ],
        compiler_params=pltpu.CompilerParams(collective_id=0, has_side_effects=True),
    )(piece)
    return jnp.moveaxis(out, 0, 1).reshape(piece.shape[0], n * piece.shape[1], piece.shape[2])


def body(tokens, trainer_q, kv_pool, prompt_kv, page_table, page_count, prompt_len):
    blk_size = lax.axis_size("blk")
    mp_size = lax.axis_size("mp")
    trainer_rows = lax.all_gather(trainer_q.astype(jnp.bfloat16), "dp", axis=1, tiled=True)
    head_weights = lax.all_gather(trainer_rows, "blk", axis=0, tiled=True)
    head_width, model_width = head_weights.shape
    block_cols = model_width // blk_size
    server_q = lax.dynamic_slice_in_dim(
        head_weights, lax.axis_index("blk") * block_cols, block_cols, axis=1
    )
    group_rows, piece_cols = tokens.shape
    own_rows = group_rows // blk_size
    pieces = tokens.reshape(blk_size, 1, own_rows, piece_cols)
    pieces = jnp.broadcast_to(pieces, (blk_size, mp_size, own_rows, piece_cols))
    pieces = pieces.reshape(blk_size * mp_size, own_rows, piece_cols)
    pieces = lax.all_to_all(pieces, ("blk", "mp"), 0, 0, tiled=True)
    token_local = jnp.transpose(pieces, (1, 0, 2)).reshape(own_rows, -1)
    queries = jnp.einsum(
        "td,hd->th", token_local, head_weights, preferred_element_type=jnp.float32
    )
    queries = queries.astype(jnp.bfloat16)
    head_count = head_width // HD
    query_heads = queries.reshape(own_rows, head_count, HD)
    length = prompt_len[0]
    row_pages = page_table[0]
    live_slots = jnp.arange(row_pages.shape[0], dtype=jnp.int32) < page_count[0]
    row_index = jnp.arange(own_rows, dtype=jnp.int32)
    own_mask = (row_index[None, :] <= row_index[:, None]) & (row_index[None, :] < length)
    softmax_state = (
        jnp.full((head_count, own_rows), -1e30, jnp.float32),
        jnp.zeros((head_count, own_rows), jnp.float32),
        jnp.zeros((head_count, own_rows, HD), jnp.float32),
    )
    softmax_state = attend_block(
        softmax_state,
        query_heads,
        prompt_kv[0].reshape(own_rows, head_count, HD),
        prompt_kv[1].reshape(own_rows, head_count, HD),
        own_mask,
    )
    shard_piece = gather_kv(kv_pool)
    key_count = shard_piece.shape[1]
    page_ids = jnp.arange(key_count, dtype=jnp.int32) // PAGE
    page_used = jnp.any((row_pages[None, :] == page_ids[:, None]) & live_slots[None, :], axis=1)
    key_mask = jnp.broadcast_to(page_used[None, :], (own_rows, key_count))
    running_max, row_total, weighted = attend_block(
        softmax_state,
        query_heads,
        shard_piece[0].reshape(key_count, head_count, HD),
        shard_piece[1].reshape(key_count, head_count, HD),
        key_mask,
    )
    mixed = weighted / row_total[:, :, None]
    mixed = jnp.where((row_index < length)[None, :, None], mixed, 0.0)
    mixed = jnp.transpose(mixed, (1, 0, 2)).reshape(own_rows, head_width).astype(jnp.bfloat16)
    return (server_q, mixed)


def solution(mesh):
    in_specs = (
        P("dp", ("blk", "mp")),
        P(("mp", "blk"), "dp"),
        P(None, ("dp", "blk"), "mp"),
        P(None, ("dp", "blk"), "mp"),
        P(("dp", "blk"), None),
        P(("dp", "blk")),
        P(("dp", "blk")),
    )
    out_specs = (P("mp", "blk"), P(("dp", "blk"), "mp"))
    return jax.shard_map(body, mesh=mesh, in_specs=in_specs, out_specs=out_specs, check_vma=False)
```

```python
import jax
import jax.numpy as jnp
from jax import lax
from jax.experimental import pallas as pl
from jax.experimental.pallas import tpu as pltpu
from jax.sharding import PartitionSpec as P

HD = 224
PAGE = 16


def attend_block(softmax_state, query_heads, key_heads, value_heads, key_mask):
    running_max, row_total, weighted = softmax_state
    scores = jnp.einsum(
        "thd,khd->htk", query_heads, key_heads, preferred_element_type=jnp.float32
    ) * HD ** (-0.5)
    scores = jnp.where(key_mask[None], scores, -1e30)
    new_max = jnp.maximum(running_max, jnp.max(scores, axis=2))
    weights = jnp.where(key_mask[None], jnp.exp(scores - new_max[:, :, None]), 0.0)
    factor = jnp.exp(running_max - new_max)
    row_total = row_total * factor + jnp.sum(weights, axis=2)
    weighted = weighted * factor[:, :, None] + jnp.einsum(
        "htk,khd->htd",
        weights.astype(jnp.bfloat16),
        value_heads,
        preferred_element_type=jnp.float32,
    )
    return (new_max, row_total, weighted)


def kv_gather_kernel(piece_ref, out_full, local_sem, send_sems, recv_sems, fwd_send, fwd_recv):
    chips = lax.axis_size("blk") // 2
    rows = piece_ref.shape[1]

    class Slots:
        def at(self, i):
            return out_full.at[:, pl.ds(i * rows, rows)]

    out_ref = Slots()
    g = lax.axis_index("dp")
    b = lax.axis_index("blk")
    m = lax.axis_index("mp")
    c = b // 2
    k = b % 2
    mate = 2 * c + 1 - k

    def peer(j):
        return (g, 2 * ((c + j) % chips) + k, m)

    def source(j):
        return 2 * ((c + chips - j) % chips) + k

    def mate_slot(j):
        return 2 * ((c + chips - j) % chips) + 1 - k

    barrier = pltpu.get_barrier_semaphore()
    for j in range(1, chips):
        pl.semaphore_signal(barrier, inc=1, device_id=peer(j), device_id_type=pl.DeviceIdType.MESH)
    pl.semaphore_signal(barrier, inc=1, device_id=(g, mate, m), device_id_type=pl.DeviceIdType.MESH)
    pl.semaphore_wait(barrier, chips)
    local = pltpu.make_async_copy(piece_ref, out_ref.at(b), local_sem)
    local.start()
    sends = []
    for j in range(1, chips):
        copy = pltpu.make_async_remote_copy(
            src_ref=piece_ref, dst_ref=out_ref.at(b), send_sem=send_sems.at[j],
            recv_sem=recv_sems.at[j], device_id=peer(j), device_id_type=pl.DeviceIdType.MESH,
        )
        copy.start()
        sends.append(copy)
    to_mate = pltpu.make_async_remote_copy(
        src_ref=piece_ref, dst_ref=out_ref.at(b), send_sem=send_sems.at[0],
        recv_sem=recv_sems.at[0], device_id=(g, mate, m), device_id_type=pl.DeviceIdType.MESH,
    )
    to_mate.start()
    forwards = []
    for j in range(1, chips):
        pltpu.make_async_remote_copy(
            src_ref=piece_ref, dst_ref=out_ref.at(source(j)), send_sem=send_sems.at[j],
            recv_sem=recv_sems.at[j], device_id=peer(j), device_id_type=pl.DeviceIdType.MESH,
        ).wait_recv()
        copy = pltpu.make_async_remote_copy(
            src_ref=out_ref.at(source(j)), dst_ref=out_ref.at(source(j)), send_sem=fwd_send.at[j],
            recv_sem=fwd_recv.at[j], device_id=(g, mate, m), device_id_type=pl.DeviceIdType.MESH,
        )
        copy.start()
        forwards.append(copy)
    local.wait()
    for copy in sends:
        copy.wait_send()
    to_mate.wait_send()
    pltpu.make_async_remote_copy(
        src_ref=piece_ref, dst_ref=out_ref.at(mate), send_sem=send_sems.at[0],
        recv_sem=recv_sems.at[0], device_id=(g, mate, m), device_id_type=pl.DeviceIdType.MESH,
    ).wait_recv()
    for copy in forwards:
        copy.wait_send()
    for j in range(1, chips):
        pltpu.make_async_remote_copy(
            src_ref=out_ref.at(mate_slot(j)), dst_ref=out_ref.at(mate_slot(j)), send_sem=fwd_send.at[j],
            recv_sem=fwd_recv.at[j], device_id=(g, mate, m), device_id_type=pl.DeviceIdType.MESH,
        ).wait_recv()


def gather_kv(piece):
    n = lax.axis_size("blk")
    chips = n // 2
    out = pl.pallas_call(
        kv_gather_kernel,
        out_shape=jax.ShapeDtypeStruct(
            (piece.shape[0], n * piece.shape[1], piece.shape[2]), piece.dtype
        ),
        in_specs=[pl.BlockSpec(memory_space=pl.ANY)],
        out_specs=pl.BlockSpec(memory_space=pl.ANY),
        scratch_shapes=[
            pltpu.SemaphoreType.DMA(()),
            pltpu.SemaphoreType.DMA((chips,)),
            pltpu.SemaphoreType.DMA((chips,)),
            pltpu.SemaphoreType.DMA((chips,)),
            pltpu.SemaphoreType.DMA((chips,)),
        ],
        compiler_params=pltpu.CompilerParams(collective_id=0, has_side_effects=True),
    )(piece)
    return out


def body(tokens, trainer_q, kv_pool, prompt_kv, page_table, page_count, prompt_len):
    blk_size = lax.axis_size("blk")
    mp_size = lax.axis_size("mp")
    group_rows, piece_cols = tokens.shape
    own_rows = group_rows // blk_size
    pieces = tokens.reshape(blk_size, 1, own_rows, piece_cols)
    pieces = jnp.broadcast_to(pieces, (blk_size, mp_size, own_rows, piece_cols))
    pieces = pieces.reshape(blk_size * mp_size, own_rows, piece_cols)
    pieces = lax.all_to_all(pieces, ("blk", "mp"), 0, 0, tiled=True)
    shard_piece = gather_kv(kv_pool)
    trainer_piece, shard_piece, pieces = lax.optimization_barrier(
        (trainer_q.astype(jnp.bfloat16), shard_piece, pieces)
    )
    trainer_rows = lax.all_gather(trainer_piece, "dp", axis=1, tiled=True)
    head_weights = lax.all_gather(trainer_rows, "blk", axis=0, tiled=True)
    head_width, model_width = head_weights.shape
    block_cols = model_width // blk_size
    server_q = lax.dynamic_slice_in_dim(
        head_weights, lax.axis_index("blk") * block_cols, block_cols, axis=1
    )
    token_local = jnp.transpose(pieces, (1, 0, 2)).reshape(own_rows, -1)
    queries = jnp.einsum(
        "td,hd->th", token_local, head_weights, preferred_element_type=jnp.float32
    )
    queries = queries.astype(jnp.bfloat16)
    head_count = head_width // HD
    query_heads = queries.reshape(own_rows, head_count, HD)
    length = prompt_len[0]
    row_pages = page_table[0]
    live_slots = jnp.arange(row_pages.shape[0], dtype=jnp.int32) < page_count[0]
    row_index = jnp.arange(own_rows, dtype=jnp.int32)
    own_mask = (row_index[None, :] <= row_index[:, None]) & (row_index[None, :] < length)
    softmax_state = (
        jnp.full((head_count, own_rows), -1e30, jnp.float32),
        jnp.zeros((head_count, own_rows), jnp.float32),
        jnp.zeros((head_count, own_rows, HD), jnp.float32),
    )
    softmax_state = attend_block(
        softmax_state,
        query_heads,
        prompt_kv[0].reshape(own_rows, head_count, HD),
        prompt_kv[1].reshape(own_rows, head_count, HD),
        own_mask,
    )
    key_count = shard_piece.shape[1]
    page_ids = jnp.arange(key_count, dtype=jnp.int32) // PAGE
    page_used = jnp.any((row_pages[None, :] == page_ids[:, None]) & live_slots[None, :], axis=1)
    key_mask = jnp.broadcast_to(page_used[None, :], (own_rows, key_count))
    running_max, row_total, weighted = attend_block(
        softmax_state,
        query_heads,
        shard_piece[0].reshape(key_count, head_count, HD),
        shard_piece[1].reshape(key_count, head_count, HD),
        key_mask,
    )
    mixed = weighted / row_total[:, :, None]
    mixed = jnp.where((row_index < length)[None, :, None], mixed, 0.0)
    mixed = jnp.transpose(mixed, (1, 0, 2)).reshape(own_rows, head_width).astype(jnp.bfloat16)
    return (server_q, mixed)


def solution(mesh):
    in_specs = (
        P("dp", ("blk", "mp")),
        P(("mp", "blk"), "dp"),
        P(None, ("dp", "blk"), "mp"),
        P(None, ("dp", "blk"), "mp"),
        P(("dp", "blk"), None),
        P(("dp", "blk")),
        P(("dp", "blk")),
    )
    out_specs = (P("mp", "blk"), P(("dp", "blk"), "mp"))
    return jax.shard_map(body, mesh=mesh, in_specs=in_specs, out_specs=out_specs, check_vma=False)
```

```python
import jax
import jax.numpy as jnp
from jax import lax
from jax.sharding import PartitionSpec as P

HD = 224
PAGE = 16


def attend_block(softmax_state, query_heads, key_heads, value_heads, key_mask):
    running_max, row_total, weighted = softmax_state
    scores = jnp.einsum(
        "thd,khd->htk", query_heads, key_heads, preferred_element_type=jnp.float32
    ) * HD ** (-0.5)
    scores = jnp.where(key_mask[None], scores, -1e30)
    new_max = jnp.maximum(running_max, jnp.max(scores, axis=2))
    weights = jnp.where(key_mask[None], jnp.exp(scores - new_max[:, :, None]), 0.0)
    factor = jnp.exp(running_max - new_max)
    row_total = row_total * factor + jnp.sum(weights, axis=2)
    weighted = weighted * factor[:, :, None] + jnp.einsum(
        "htk,khd->htd",
        weights.astype(jnp.bfloat16),
        value_heads,
        preferred_element_type=jnp.float32,
    )
    return (new_max, row_total, weighted)


def body(tokens, trainer_q, kv_pool, prompt_kv, page_table, page_count, prompt_len):
    blk_size = lax.axis_size("blk")
    mp_size = lax.axis_size("mp")
    dp_size = lax.axis_size("dp")
    g = lax.axis_index("dp")
    own_piece = trainer_q.astype(jnp.bfloat16)
    received = jnp.stack(
        [own_piece]
        + [
            lax.ppermute(own_piece, "dp", [(i, (i + j) % dp_size) for i in range(dp_size)])
            for j in range(1, dp_size)
        ]
    )
    ordered = jnp.take(received, (g - jnp.arange(dp_size)) % dp_size, axis=0)
    trainer_rows = jnp.transpose(ordered, (1, 0, 2)).reshape(own_piece.shape[0], -1)
    head_weights = lax.all_gather(trainer_rows, "blk", axis=0, tiled=True)
    head_width, model_width = head_weights.shape
    block_cols = model_width // blk_size
    server_q = lax.dynamic_slice_in_dim(
        head_weights, lax.axis_index("blk") * block_cols, block_cols, axis=1
    )
    group_rows, piece_cols = tokens.shape
    own_rows = group_rows // blk_size
    pieces = tokens.reshape(blk_size, 1, own_rows, piece_cols)
    pieces = jnp.broadcast_to(pieces, (blk_size, mp_size, own_rows, piece_cols))
    pieces = pieces.reshape(blk_size * mp_size, own_rows, piece_cols)
    pieces = lax.all_to_all(pieces, ("blk", "mp"), 0, 0, tiled=True)
    token_local = jnp.transpose(pieces, (1, 0, 2)).reshape(own_rows, -1)
    queries = jnp.einsum(
        "td,hd->th", token_local, head_weights, preferred_element_type=jnp.float32
    )
    queries = queries.astype(jnp.bfloat16)
    head_count = head_width // HD
    query_heads = queries.reshape(own_rows, head_count, HD)
    length = prompt_len[0]
    row_pages = page_table[0]
    live_slots = jnp.arange(row_pages.shape[0], dtype=jnp.int32) < page_count[0]
    row_index = jnp.arange(own_rows, dtype=jnp.int32)
    own_mask = (row_index[None, :] <= row_index[:, None]) & (row_index[None, :] < length)
    softmax_state = (
        jnp.full((head_count, own_rows), -1e30, jnp.float32),
        jnp.zeros((head_count, own_rows), jnp.float32),
        jnp.zeros((head_count, own_rows, HD), jnp.float32),
    )
    softmax_state = attend_block(
        softmax_state,
        query_heads,
        prompt_kv[0].reshape(own_rows, head_count, HD),
        prompt_kv[1].reshape(own_rows, head_count, HD),
        own_mask,
    )
    shard_piece = lax.all_gather(kv_pool, "blk", axis=1, tiled=True)
    key_count = shard_piece.shape[1]
    page_ids = jnp.arange(key_count, dtype=jnp.int32) // PAGE
    page_used = jnp.any((row_pages[None, :] == page_ids[:, None]) & live_slots[None, :], axis=1)
    key_mask = jnp.broadcast_to(page_used[None, :], (own_rows, key_count))
    running_max, row_total, weighted = attend_block(
        softmax_state,
        query_heads,
        shard_piece[0].reshape(key_count, head_count, HD),
        shard_piece[1].reshape(key_count, head_count, HD),
        key_mask,
    )
    mixed = weighted / row_total[:, :, None]
    mixed = jnp.where((row_index < length)[None, :, None], mixed, 0.0)
    mixed = jnp.transpose(mixed, (1, 0, 2)).reshape(own_rows, head_width).astype(jnp.bfloat16)
    return (server_q, mixed)


def solution(mesh):
    in_specs = (
        P("dp", ("blk", "mp")),
        P(("mp", "blk"), "dp"),
        P(None, ("dp", "blk"), "mp"),
        P(None, ("dp", "blk"), "mp"),
        P(("dp", "blk"), None),
        P(("dp", "blk")),
        P(("dp", "blk")),
    )
    out_specs = (P("mp", "blk"), P(("dp", "blk"), "mp"))
    return jax.shard_map(body, mesh=mesh, in_specs=in_specs, out_specs=out_specs, check_vma=False)
```

```python
import jax
import jax.numpy as jnp
from jax import lax
from jax.sharding import PartitionSpec as P

HD = 224
PAGE = 16


def attend_block(softmax_state, query_heads, key_heads, value_heads, key_mask):
    running_max, row_total, weighted = softmax_state
    scores = jnp.einsum(
        "thd,khd->htk", query_heads, key_heads, preferred_element_type=jnp.float32
    ) * HD ** (-0.5)
    scores = jnp.where(key_mask[None], scores, -1e30)
    new_max = jnp.maximum(running_max, jnp.max(scores, axis=2))
    weights = jnp.where(key_mask[None], jnp.exp(scores - new_max[:, :, None]), 0.0)
    factor = jnp.exp(running_max - new_max)
    row_total = row_total * factor + jnp.sum(weights, axis=2)
    weighted = weighted * factor[:, :, None] + jnp.einsum(
        "htk,khd->htd",
        weights.astype(jnp.bfloat16),
        value_heads,
        preferred_element_type=jnp.float32,
    )
    return (new_max, row_total, weighted)


def body(tokens, trainer_q, kv_pool, prompt_kv, page_table, page_count, prompt_len):
    blk_size = lax.axis_size("blk")
    mp_size = lax.axis_size("mp")
    dp_size = lax.axis_size("dp")
    g = lax.axis_index("dp")
    group_rows, piece_cols = tokens.shape
    own_rows = group_rows // blk_size
    pieces = tokens.reshape(blk_size, 1, own_rows, piece_cols)
    pieces = jnp.broadcast_to(pieces, (blk_size, mp_size, own_rows, piece_cols))
    pieces = pieces.reshape(blk_size * mp_size, own_rows, piece_cols)
    own_piece, pieces = lax.optimization_barrier((trainer_q.astype(jnp.bfloat16), pieces))
    received = jnp.stack(
        [own_piece]
        + [
            lax.ppermute(own_piece, "dp", [(i, (i + j) % dp_size) for i in range(dp_size)])
            for j in range(1, dp_size)
        ]
    )
    ordered = jnp.take(received, (g - jnp.arange(dp_size)) % dp_size, axis=0)
    trainer_rows = jnp.transpose(ordered, (1, 0, 2)).reshape(own_piece.shape[0], -1)
    head_weights = lax.all_gather(trainer_rows, "blk", axis=0, tiled=True)
    head_width, model_width = head_weights.shape
    block_cols = model_width // blk_size
    server_q = lax.dynamic_slice_in_dim(
        head_weights, lax.axis_index("blk") * block_cols, block_cols, axis=1
    )
    pieces = lax.all_to_all(pieces, ("blk", "mp"), 0, 0, tiled=True)
    token_local = jnp.transpose(pieces, (1, 0, 2)).reshape(own_rows, -1)
    queries = jnp.einsum(
        "td,hd->th", token_local, head_weights, preferred_element_type=jnp.float32
    )
    queries = queries.astype(jnp.bfloat16)
    head_count = head_width // HD
    query_heads = queries.reshape(own_rows, head_count, HD)
    length = prompt_len[0]
    row_pages = page_table[0]
    live_slots = jnp.arange(row_pages.shape[0], dtype=jnp.int32) < page_count[0]
    row_index = jnp.arange(own_rows, dtype=jnp.int32)
    own_mask = (row_index[None, :] <= row_index[:, None]) & (row_index[None, :] < length)
    softmax_state = (
        jnp.full((head_count, own_rows), -1e30, jnp.float32),
        jnp.zeros((head_count, own_rows), jnp.float32),
        jnp.zeros((head_count, own_rows, HD), jnp.float32),
    )
    softmax_state = attend_block(
        softmax_state,
        query_heads,
        prompt_kv[0].reshape(own_rows, head_count, HD),
        prompt_kv[1].reshape(own_rows, head_count, HD),
        own_mask,
    )
    shard_piece = lax.all_gather(kv_pool, "blk", axis=1, tiled=True)
    key_count = shard_piece.shape[1]
    page_ids = jnp.arange(key_count, dtype=jnp.int32) // PAGE
    page_used = jnp.any((row_pages[None, :] == page_ids[:, None]) & live_slots[None, :], axis=1)
    key_mask = jnp.broadcast_to(page_used[None, :], (own_rows, key_count))
    running_max, row_total, weighted = attend_block(
        softmax_state,
        query_heads,
        shard_piece[0].reshape(key_count, head_count, HD),
        shard_piece[1].reshape(key_count, head_count, HD),
        key_mask,
    )
    mixed = weighted / row_total[:, :, None]
    mixed = jnp.where((row_index < length)[None, :, None], mixed, 0.0)
    mixed = jnp.transpose(mixed, (1, 0, 2)).reshape(own_rows, head_width).astype(jnp.bfloat16)
    return (server_q, mixed)


def solution(mesh):
    in_specs = (
        P("dp", ("blk", "mp")),
        P(("mp", "blk"), "dp"),
        P(None, ("dp", "blk"), "mp"),
        P(None, ("dp", "blk"), "mp"),
        P(("dp", "blk"), None),
        P(("dp", "blk")),
        P(("dp", "blk")),
    )
    out_specs = (P("mp", "blk"), P(("dp", "blk"), "mp"))
    return jax.shard_map(body, mesh=mesh, in_specs=in_specs, out_specs=out_specs, check_vma=False)
```

```python
import jax
import jax.numpy as jnp
from jax import lax
from jax.sharding import PartitionSpec as P

HD = 224
PAGE = 16


def attend_block(softmax_state, query_heads, key_heads, value_heads, key_mask):
    running_max, row_total, weighted = softmax_state
    scores = jnp.einsum(
        "thd,khd->htk", query_heads, key_heads, preferred_element_type=jnp.float32
    ) * HD ** (-0.5)
    scores = jnp.where(key_mask[None], scores, -1e30)
    new_max = jnp.maximum(running_max, jnp.max(scores, axis=2))
    weights = jnp.where(key_mask[None], jnp.exp(scores - new_max[:, :, None]), 0.0)
    factor = jnp.exp(running_max - new_max)
    row_total = row_total * factor + jnp.sum(weights, axis=2)
    weighted = weighted * factor[:, :, None] + jnp.einsum(
        "htk,khd->htd",
        weights.astype(jnp.bfloat16),
        value_heads,
        preferred_element_type=jnp.float32,
    )
    return (new_max, row_total, weighted)


def body(tokens, trainer_q, kv_pool, prompt_kv, page_table, page_count, prompt_len):
    blk_size = lax.axis_size("blk")
    mp_size = lax.axis_size("mp")
    dp_size = lax.axis_size("dp")
    g = lax.axis_index("dp")
    own_piece = trainer_q.astype(jnp.bfloat16)
    received = jnp.stack(
        [own_piece]
        + [
            lax.ppermute(own_piece, "dp", [(i, (i + j) % dp_size) for i in range(dp_size)])
            for j in range(1, dp_size)
        ]
    )
    ordered = jnp.take(received, (g - jnp.arange(dp_size)) % dp_size, axis=0)
    trainer_rows = jnp.transpose(ordered, (1, 0, 2)).reshape(own_piece.shape[0], -1)
    head_weights = lax.all_gather(trainer_rows, "blk", axis=0, tiled=True)
    head_width, model_width = head_weights.shape
    block_cols = model_width // blk_size
    server_q = lax.dynamic_slice_in_dim(
        head_weights, lax.axis_index("blk") * block_cols, block_cols, axis=1
    )
    group_rows, piece_cols = tokens.shape
    own_rows = group_rows // blk_size
    pieces = tokens.reshape(blk_size, 1, own_rows, piece_cols)
    pieces = jnp.broadcast_to(pieces, (blk_size, mp_size, own_rows, piece_cols))
    pieces = pieces.reshape(blk_size * mp_size, own_rows, piece_cols)
    pieces = lax.all_to_all(pieces, ("blk", "mp"), 0, 0, tiled=True)
    token_local = jnp.transpose(pieces, (1, 0, 2)).reshape(own_rows, -1)
    queries = jnp.einsum(
        "td,hd->th", token_local, head_weights, preferred_element_type=jnp.float32
    )
    queries = queries.astype(jnp.bfloat16)
    head_count = head_width // HD
    length = prompt_len[0]
    row_pages = page_table[0]
    live_slots = jnp.arange(row_pages.shape[0], dtype=jnp.int32) < page_count[0]
    row_index = jnp.arange(own_rows, dtype=jnp.int32)
    own_mask = (row_index[None, :] <= row_index[:, None]) & (row_index[None, :] < length)
    shard_piece = lax.all_gather(kv_pool, "blk", axis=1, tiled=True)
    key_count = shard_piece.shape[1]
    page_ids = jnp.arange(key_count, dtype=jnp.int32) // PAGE
    page_used = jnp.any((row_pages[None, :] == page_ids[:, None]) & live_slots[None, :], axis=1)
    key_mask = jnp.concatenate(
        [own_mask, jnp.broadcast_to(page_used[None, :], (own_rows, key_count))], axis=1
    )
    outputs = []
    for h in range(head_count):
        cols = slice(h * HD, (h + 1) * HD)
        query_h = queries[:, cols]
        keys_h = jnp.concatenate([prompt_kv[0][:, cols], shard_piece[0][:, cols]], axis=0)
        values_h = jnp.concatenate([prompt_kv[1][:, cols], shard_piece[1][:, cols]], axis=0)
        scores = lax.dot_general(
            query_h, keys_h, (((1,), (1,)), ((), ())), preferred_element_type=jnp.float32
        ) * HD ** (-0.5)
        scores = jnp.where(key_mask, scores, -1e30)
        largest = jnp.max(scores, axis=1, keepdims=True)
        weights = jnp.where(key_mask, jnp.exp(scores - largest), 0.0)
        row_total = jnp.sum(weights, axis=1, keepdims=True)
        mixed = jnp.dot(
            weights.astype(jnp.bfloat16), values_h, preferred_element_type=jnp.float32
        ) / row_total
        outputs.append(jnp.where((row_index < length)[:, None], mixed, 0.0))
    mixed = jnp.concatenate(outputs, axis=1).astype(jnp.bfloat16)
    return (server_q, mixed)


def solution(mesh):
    in_specs = (
        P("dp", ("blk", "mp")),
        P(("mp", "blk"), "dp"),
        P(None, ("dp", "blk"), "mp"),
        P(None, ("dp", "blk"), "mp"),
        P(("dp", "blk"), None),
        P(("dp", "blk")),
        P(("dp", "blk")),
    )
    out_specs = (P("mp", "blk"), P(("dp", "blk"), "mp"))
    return jax.shard_map(body, mesh=mesh, in_specs=in_specs, out_specs=out_specs, check_vma=False)
```

```python
import jax
import jax.numpy as jnp
from jax import lax
from jax.sharding import PartitionSpec as P

HD = 224
PAGE = 16


def attend_block(softmax_state, query_heads, key_heads, value_heads, key_mask):
    running_max, row_total, weighted = softmax_state
    scores = jnp.einsum(
        "thd,khd->htk", query_heads, key_heads, preferred_element_type=jnp.float32
    ) * HD ** (-0.5)
    scores = jnp.where(key_mask[None], scores, -1e30)
    new_max = jnp.maximum(running_max, jnp.max(scores, axis=2))
    weights = jnp.where(key_mask[None], jnp.exp(scores - new_max[:, :, None]), 0.0)
    factor = jnp.exp(running_max - new_max)
    row_total = row_total * factor + jnp.sum(weights, axis=2)
    weighted = weighted * factor[:, :, None] + jnp.einsum(
        "htk,khd->htd",
        weights.astype(jnp.bfloat16),
        value_heads,
        preferred_element_type=jnp.float32,
    )
    return (new_max, row_total, weighted)


def body(tokens, trainer_q, kv_pool, prompt_kv, page_table, page_count, prompt_len):
    blk_size = lax.axis_size("blk")
    mp_size = lax.axis_size("mp")
    dp_size = lax.axis_size("dp")
    g = lax.axis_index("dp")
    own_piece = trainer_q.astype(jnp.bfloat16)
    received = jnp.stack(
        [own_piece]
        + [
            lax.ppermute(own_piece, "dp", [(i, (i + j) % dp_size) for i in range(dp_size)])
            for j in range(1, dp_size)
        ]
    )
    ordered = jnp.take(received, (g - jnp.arange(dp_size)) % dp_size, axis=0)
    trainer_rows = jnp.transpose(ordered, (1, 0, 2)).reshape(own_piece.shape[0], -1)
    head_weights = lax.all_gather(trainer_rows, "blk", axis=0, tiled=True)
    head_width, model_width = head_weights.shape
    block_cols = model_width // blk_size
    piece_rows = trainer_rows.shape[0]
    outgoing = jnp.transpose(trainer_rows.reshape(piece_rows, blk_size, block_cols), (1, 0, 2))
    server_q = lax.all_to_all(outgoing, "blk", 0, 0, tiled=True).reshape(head_width, block_cols)
    group_rows, piece_cols = tokens.shape
    own_rows = group_rows // blk_size
    pieces = tokens.reshape(blk_size, 1, own_rows, piece_cols)
    pieces = jnp.broadcast_to(pieces, (blk_size, mp_size, own_rows, piece_cols))
    pieces = pieces.reshape(blk_size * mp_size, own_rows, piece_cols)
    pieces = lax.all_to_all(pieces, ("blk", "mp"), 0, 0, tiled=True)
    token_local = jnp.transpose(pieces, (1, 0, 2)).reshape(own_rows, -1)
    queries = jnp.einsum(
        "td,hd->th", token_local, head_weights, preferred_element_type=jnp.float32
    )
    queries = queries.astype(jnp.bfloat16)
    head_count = head_width // HD
    query_heads = queries.reshape(own_rows, head_count, HD)
    length = prompt_len[0]
    row_pages = page_table[0]
    live_slots = jnp.arange(row_pages.shape[0], dtype=jnp.int32) < page_count[0]
    row_index = jnp.arange(own_rows, dtype=jnp.int32)
    own_mask = (row_index[None, :] <= row_index[:, None]) & (row_index[None, :] < length)
    softmax_state = (
        jnp.full((head_count, own_rows), -1e30, jnp.float32),
        jnp.zeros((head_count, own_rows), jnp.float32),
        jnp.zeros((head_count, own_rows, HD), jnp.float32),
    )
    softmax_state = attend_block(
        softmax_state,
        query_heads,
        prompt_kv[0].reshape(own_rows, head_count, HD),
        prompt_kv[1].reshape(own_rows, head_count, HD),
        own_mask,
    )
    shard_piece = lax.all_gather(kv_pool, "blk", axis=1, tiled=True)
    key_count = shard_piece.shape[1]
    page_ids = jnp.arange(key_count, dtype=jnp.int32) // PAGE
    page_used = jnp.any((row_pages[None, :] == page_ids[:, None]) & live_slots[None, :], axis=1)
    key_mask = jnp.broadcast_to(page_used[None, :], (own_rows, key_count))
    running_max, row_total, weighted = attend_block(
        softmax_state,
        query_heads,
        shard_piece[0].reshape(key_count, head_count, HD),
        shard_piece[1].reshape(key_count, head_count, HD),
        key_mask,
    )
    mixed = weighted / row_total[:, :, None]
    mixed = jnp.where((row_index < length)[None, :, None], mixed, 0.0)
    mixed = jnp.transpose(mixed, (1, 0, 2)).reshape(own_rows, head_width).astype(jnp.bfloat16)
    return (server_q, mixed)


def solution(mesh):
    in_specs = (
        P("dp", ("blk", "mp")),
        P(("mp", "blk"), "dp"),
        P(None, ("dp", "blk"), "mp"),
        P(None, ("dp", "blk"), "mp"),
        P(("dp", "blk"), None),
        P(("dp", "blk")),
        P(("dp", "blk")),
    )
    out_specs = (P("mp", "blk"), P(("dp", "blk"), "mp"))
    return jax.shard_map(body, mesh=mesh, in_specs=in_specs, out_specs=out_specs, check_vma=False)
```
